256 devices in a mesh: frames: 16 (over z, core), rows: 16 (over y, x).
Axes of the slice: x: 4, y: 4, z: 8, core: 2. Of those that a mesh axis runs over, the one named last changes fastest.
Arguments:
- observed: bfloat16 [64, 1, 256, 2048], P('frames', None, 'rows'), may hold values from -6 to 6
- history: bfloat16 [127, 1, 256, 2048], P(None, None, 'rows', 'frames'), may hold values from 0 to 0.3984375
- spikes_start: float32 [64, 1, 256, 2048], P('frames', None, 'rows'), may hold values from 0 to 0.4
- kernel: bfloat16 [128], replicated, may hold values from 0 to 1, as said below
- smooth_half: float32 [8], replicated, may hold values from 0.2 to 1
Outputs:
- spikes: float32 [64, 1, 256, 2048], P('frames', None, 'rows')
- point: float32 [64, 1, 256, 2048], P('frames', None, 'rows')
The draws below stay inside these ranges and needn't reach their ends.
Inputs may be any that keep to these rules, and one draw needn't show every extreme that they name: kernel taps are positive and fall roughly exponentially over the lags.
All inputs are finite; a program needn't handle non-finite values.
Results may differ from the reference program's by a relative error of at most 0.0012.
The reference program's roundings to bfloat16 on the way count: a program that leaves them out, or rounds other values in their place, can miss the bound.
Values may be sent and summed in bfloat16 or wider, within the bound.
A program may use at most 64 MiB of HBM per device.

```python
import math
import jax
import jax.numpy as jnp
from jax import lax

FRAMES = 64
PLANES = 1
COLS = 2048
TAPS = 128
ITERS = 2
HALF = 8
HIST = 127
ROWS = 256


def draw_kernel(key, part):
    lags = jnp.arange(TAPS, dtype=jnp.float32)
    rough = jax.random.uniform(key, (TAPS,), jnp.float32, 0.5, 1.5)
    values = 7.0 / TAPS * jnp.exp(-2.0 * lags / TAPS) * rough
    return values.astype(jnp.bfloat16)


def level_of(key, shape, pieces, least, top_value):
    gain, own = 1.0, jax.random.fold_in(key, 6)
    for axis_at, blocks in pieces:
        steps = jnp.exp(jax.random.uniform(jax.random.fold_in(own, axis_at), (blocks,), jnp.float32, least / len(pieces), top_value / len(pieces)))
        gain = gain * jnp.repeat(steps, shape[axis_at] // blocks).reshape([-1 if axis == axis_at else 1 for axis in range(len(shape))])
    return gain


def gaussian(key, dims, scale, limit, split=(), kind=jnp.bfloat16):
    values = scale * jax.random.normal(key, dims, jnp.float32)
    if split:
        values = values * level_of(key, dims, split, -0.22, 0.18)
    return jnp.clip(values, -limit, limit).astype(kind)


def setup_inputs(seed: int = 0) -> dict:
    key_list = jax.random.split(jax.random.key(seed), 6)
    return {
        "observed": gaussian(key_list[0], (FRAMES, PLANES, ROWS, COLS), 1.0, 6.0, ((0, 16), (2, 16))),
        "history": jnp.clip(0.3984375 * jax.random.uniform(key_list[1], (HIST, PLANES, ROWS, COLS), jnp.float32) ** level_of(key_list[1], (HIST, PLANES, ROWS, COLS), ((2, 16), (3, 16)), -0.2, 0.2), 0.0, 0.3984375).astype(jnp.bfloat16),
        "spikes_start": jnp.clip(0.4 * jax.random.uniform(key_list[2], (FRAMES, PLANES, ROWS, COLS), jnp.float32) ** level_of(key_list[2], (FRAMES, PLANES, ROWS, COLS), ((0, 16), (2, 16)), -0.2, 0.2), 0.0, 0.4),
        "kernel": draw_kernel(jax.random.fold_in(key_list[5], 71), 0),
        "smooth_half": jnp.clip(jnp.exp(jax.random.uniform(key_list[4], (HALF,), jnp.float32, math.log(0.2), math.log(1.0))), 0.2, 1.0),
    }


REG_WEIGHT = 4.0
SPARSE_WEIGHT = 0.1

def momentum_terms(count):
    current = 1.0
    terms = []
    for iteration in range(count):
        upcoming = (1.0 + math.sqrt(1.0 + 4.0 * current * current)) / 2.0
        terms.append((current - 1.0) / upcoming)
        current = upcoming
    return terms

def full_taps(smooth_half):
    mirrored = jnp.concatenate([smooth_half[::-1], smooth_half[1:]])
    return mirrored / jnp.sum(mirrored)

def smooth_padded(padded, smooth_taps):
    length = smooth_taps.shape[0]
    rim_width = (length - 1) // 2
    out_rows = padded.shape[2] - 2 * rim_width
    out_cols = padded.shape[3] - 2 * rim_width
    across = smooth_taps[0] * padded[:, :, 0:out_rows, :]
    for offset in range(1, length):
        across = across + smooth_taps[offset] * padded[:, :, offset:offset + out_rows, :]
    result = smooth_taps[0] * across[:, :, :, 0:out_cols]
    for offset in range(1, length):
        result = result + smooth_taps[offset] * across[:, :, :, offset:offset + out_cols]
    return result

def smooth_field(field_bf, smooth_taps):
    rim_width = (smooth_taps.shape[0] - 1) // 2
    padded = jnp.pad(field_bf.astype(jnp.float32), ((0, 0), (0, 0), (rim_width, rim_width), (rim_width, rim_width)))
    return smooth_padded(padded, smooth_taps)

def toeplitz_matrix(kernel, frame_count):
    length = kernel.shape[0]
    lags = jnp.arange(frame_count, dtype=jnp.int32)[:, None] + (length - 1) - jnp.arange(frame_count + length - 1, dtype=jnp.int32)[None, :]
    onehot = lags[:, :, None] == jnp.arange(length, dtype=jnp.int32)[None, None, :]
    picked = jnp.where(onehot, kernel.astype(jnp.float32)[None, None, :], jnp.float32(0.0))
    return lax.optimization_barrier(jnp.sum(picked, axis=2)).astype(jnp.bfloat16)

def convolve_full(toeplitz_mat, history, point_bf):
    extended = jnp.concatenate([history, point_bf], axis=0)
    flat = extended.reshape(extended.shape[0], -1)
    return jnp.dot(toeplitz_mat, flat, preferred_element_type=jnp.float32).reshape(point_bf.shape)

def convolve_adjoint(window_mat, resid_bf):
    flat = resid_bf.reshape(resid_bf.shape[0], -1)
    return jnp.dot(window_mat.T, flat, preferred_element_type=jnp.float32).reshape(resid_bf.shape)

def convolve_window(window_mat, grad_bf):
    flat = grad_bf.reshape(grad_bf.shape[0], -1)
    return jnp.dot(window_mat, flat, preferred_element_type=jnp.float32).reshape(grad_bf.shape)

def reference(observed, history, spikes_start, kernel, smooth_half):
    smooth_taps = full_taps(smooth_half)
    toeplitz_mat = toeplitz_matrix(kernel, observed.shape[0])
    window_mat = toeplitz_mat[:, kernel.shape[0] - 1:]
    previous = spikes_start
    point = spikes_start
    for beta in momentum_terms(ITERS):
        point_bf = lax.optimization_barrier(point.astype(jnp.bfloat16))
        resid_bf = (convolve_full(toeplitz_mat, history, point_bf) - observed.astype(jnp.float32)).astype(jnp.bfloat16)
        resid_bf = lax.optimization_barrier(resid_bf)
        back_bf = lax.optimization_barrier(convolve_adjoint(window_mat, resid_bf).astype(jnp.bfloat16))
        gradient = back_bf.astype(jnp.float32) + REG_WEIGHT * (point_bf.astype(jnp.float32) - smooth_field(point_bf, smooth_taps))
        grad_bf = lax.optimization_barrier(gradient.astype(jnp.bfloat16))
        grad_f = grad_bf.astype(jnp.float32)
        grad_norm = jnp.sum(gradient * gradient)
        smooth_curv = jnp.sum(grad_f * (grad_f - smooth_field(grad_bf, smooth_taps)))
        conv_grad = convolve_window(window_mat, grad_bf)
        conv_curv = jnp.sum(conv_grad * conv_grad)
        step_size = grad_norm / (conv_curv + REG_WEIGHT * smooth_curv)
        updated = jnp.maximum(point - step_size * gradient - step_size * SPARSE_WEIGHT, 0.0)
        point = updated + beta * (updated - previous)
        previous = updated
    return (previous, point)
```

```python
import functools
import math

import jax
import jax.numpy as jnp
from jax import lax
from jax.experimental import pallas as pl
from jax.experimental.pallas import tpu as pltpu
from jax.sharding import PartitionSpec as P

ITERS = 2
REG_WEIGHT = 4.0
SPARSE_WEIGHT = 0.1
MESH = pl.DeviceIdType.MESH
F32 = jnp.float32
BF16 = jnp.bfloat16
GROUPS = 8


def momentum_terms(count):
    current = 1.0
    terms = []
    for iteration in range(count):
        upcoming = (1.0 + math.sqrt(1.0 + 4.0 * current * current)) / 2.0
        terms.append((current - 1.0) / upcoming)
        current = upcoming
    return terms


def iota(shape, dim):
    return lax.broadcasted_iota(jnp.int32, shape, dim)


def dot(a, b):
    return jnp.dot(a, b, preferred_element_type=F32)


def onehot(cond):
    return jnp.where(cond, 1.0, 0.0).astype(BF16)


def split(value):
    high = value.astype(BF16)
    return high, (value - high.astype(F32)).astype(BF16)


def body(
    nf,
    nr,
    frames,
    obs_hbm,
    hist_hbm,
    start_hbm,
    taps_ref,
    half_ref,
    out_spikes,
    out_point,
    start_f,
    hi_f,
    lo_f,
    hi_c,
    lo_c,
    obs_c,
    hist_v,
    grad_c,
    grad_f,
    edge_s,
    strip_s,
    above,
    below,
    strips,
    row_s,
    row_r,
    kh,
    kw,
    kwt,
    band,
    ah,
    al,
    sel,
    hbh,
    hbl,
    local_sems,
    a2a_send,
    a2a_recv,
    halo_send,
    halo_recv,
    sum_send,
    sum_recv,
):
    col = lax.axis_index("frames")
    row = lax.axis_index("rows")
    per = frames // nf
    rows = frames * 8
    hist_len = hist_hbm.shape[0]
    tap_count = taps_ref.shape[1]

    load_start = pltpu.make_async_copy(start_hbm, start_f, local_sems.at[0])
    load_start.start()
    load_hist = pltpu.make_async_copy(hist_hbm, hist_v.at[pl.ds(0, hist_len)], local_sems.at[1])
    load_hist.start()

    above[...] = jnp.zeros(above.shape, BF16)
    below[...] = jnp.zeros(below.shape, BF16)
    strips[...] = jnp.zeros(strips.shape, BF16)
    hist_v[hist_len:] = jnp.zeros((hist_v.shape[0] - hist_len,) + hist_v.shape[1:], BF16)

    barrier = pltpu.get_barrier_semaphore()

    def signal_frames(k, carry):
        pl.semaphore_signal(
            barrier, inc=1, device_id={"frames": lax.rem(col + k, nf)}, device_id_type=MESH
        )
        return carry

    def signal_rows(k, carry):
        pl.semaphore_signal(
            barrier, inc=1, device_id={"rows": lax.rem(row + k, nr)}, device_id_type=MESH
        )
        return carry

    lax.fori_loop(1, nf, signal_frames, 0)
    lax.fori_loop(1, nr, signal_rows, 0)
    exists = {}
    for dc in (-1, 0, 1):
        for dr in (-1, 0, 1):
            conds = []
            if dc == -1:
                conds.append(col > 0)
            if dc == 1:
                conds.append(col < nf - 1)
            if dr == -1:
                conds.append(row > 0)
            if dr == 1:
                conds.append(row < nr - 1)
            if conds:
                exists[dc, dr] = functools.reduce(jnp.logical_and, conds)
    for dc in (-1, 1):
        for dr in (-1, 1):

            @pl.when(exists[dc, dr])
            def _():
                pl.semaphore_signal(
                    barrier,
                    inc=1,
                    device_id={"frames": col + dc, "rows": row + dr},
                    device_id_type=MESH,
                )

    load_start.wait()
    for c in range(nf):
        high, low = split(start_f[:, :, :, c * 128 : (c + 1) * 128])
        hi_f[c] = high
        lo_f[c] = low

    sides = (col > 0).astype(jnp.int32) + (col < nf - 1).astype(jnp.int32)
    ends = (row > 0).astype(jnp.int32) + (row < nr - 1).astype(jnp.int32)
    pl.semaphore_wait(barrier, (nf - 1) + (nr - 1) + sides * ends)

    def order(k):
        return nf // 2 + ((k + 1) // 2) * (1 - 2 * lax.rem(k, 2))

    def exchange(index, source, target, own_source, own_target):
        own = pltpu.make_async_copy(own_source, own_target, a2a_recv.at[index])
        own.start()

        def send(k, carry):
            peer = lax.rem(col + order(k), nf)
            pltpu.make_async_remote_copy(
                src_ref=source(peer),
                dst_ref=target,
                send_sem=a2a_send.at[index],
                recv_sem=a2a_recv.at[index],
                device_id={"frames": peer},
                device_id_type=MESH,
            ).start()
            return carry

        lax.fori_loop(0, nf - 1, send, 0)

    def wait_bytes(view, sem):
        pltpu.make_async_copy(view, view, sem).wait()

    def to_block(index, source, buffer):
        target = buffer.at[pl.ds(col * per, per)]
        exchange(index, source, target, source(col), target)

    to_block(0, lambda c: hi_f.at[c], hi_c)
    to_block(1, lambda c: obs_hbm.at[:, :, :, pl.ds(pl.multiple_of(c * 128, 128), 128)], obs_c)
    to_block(2, lambda c: lo_f.at[c], lo_c)

    def gradient_out(it):
        target = grad_f.at[it, col]
        exchange(
            3 + it,
            lambda f: grad_c.at[it, pl.ds(f * per, per)],
            target,
            grad_c.at[it, pl.ds(col * per, per)],
            target,
        )

    size = 256
    spread = jnp.concatenate(
        [taps_ref[...].astype(F32), jnp.zeros((1, size - tap_count), F32)], axis=1
    )
    spread = jnp.broadcast_to(spread, (size, size))
    shifted = pltpu.roll(spread, size - (tap_count - 1), 1, stride=1, stride_axis=0).astype(BF16)
    at_t = onehot(iota((rows, size), 0) // 8 == iota((rows, size), 1))
    by_s = lax.dot_general(
        at_t, shifted, (((1,), (1,)), ((), ())), preferred_element_type=F32
    ).astype(BF16)

    def same_row(shape):
        return lax.rem(iota(shape, 0), 8) == lax.rem(iota(shape, 1), 8)

    hist_cols = kh.shape[1]
    s_of = iota((size, hist_cols), 0)
    pick = onehot((s_of == iota((size, hist_cols), 1) // 8) & (s_of < hist_len))
    kh[...] = jnp.where(same_row((rows, hist_cols)), dot(by_s, pick), 0.0).astype(BF16)
    pick = onehot(iota((size, rows), 0) == iota((size, rows), 1) // 8 + hist_len)
    kw[...] = jnp.where(same_row((rows, rows)), dot(by_s, pick), 0.0).astype(BF16)
    at_s = onehot(iota((rows, size), 0) // 8 + hist_len == iota((rows, size), 1))
    by_t = dot(at_s, shifted).astype(BF16)
    pick = onehot(iota((size, rows), 0) == iota((size, rows), 1) // 8)
    kwt[...] = jnp.where(same_row((rows, rows)), dot(by_t, pick), 0.0).astype(BF16)

    half = [half_ref[k] for k in range(half_ref.shape[0])]
    reach = half_ref.shape[0] - 1
    total = half[0]
    for k in range(1, reach + 1):
        total = total + 2.0 * half[k]
    total = jnp.full((1, 1), total, F32)
    scale = 1.0 / (total * total)

    def taps_at(distance):
        value = jnp.zeros(distance.shape, F32)
        for k in range(reach + 1):
            value = jnp.where(distance == k, half[k], value)
        return value

    high, low = split(taps_at(jnp.abs(iota((128, 128), 0) - iota((128, 128), 1))))
    band[:, 0:128] = high
    band[:, 128:256] = low

    rg = ah.shape[0]
    i0, i1 = iota((rg, rg), 0), iota((rg, rg), 1)
    for d in (-1, 0, 1):
        near = taps_at(jnp.abs(8 * d + lax.rem(i1, 8) - lax.rem(i0, 8)))
        high, low = split(jnp.where(i0 // 8 == i1 // 8, near, 0.0))
        ah[:, (d + 1) * rg : (d + 2) * rg] = high
        al[:, (d + 1) * rg : (d + 2) * rg] = low

    k0, k1 = iota((256, 256), 0), iota((256, 256), 1)
    place = lax.rem(k0, 128)
    inner, line = lax.rem(place, 8), lax.rem(k1, 128)
    near = taps_at(jnp.where(k0 < 128, line + 8 - inner, 128 + inner - line))
    near = jnp.where(lax.rem(place // 8, 2) == k1 // 128, near, 0.0)
    for g in range(GROUPS):
        high, low = split(jnp.where(place // 16 == g, near, 0.0))
        hbh[:, g * 256 : (g + 1) * 256] = high
        hbl[:, g * 256 : (g + 1) * 256] = low
    place = lax.rem(k1, 128)
    inner, line = lax.rem(place, 8), lax.rem(k0, 128)
    chosen = (lax.rem(place // 8, 2) == k0 // 128) & (line == jnp.where(k1 < 128, 120 + inner, inner))
    for g in range(GROUPS):
        sel[g * 256 : (g + 1) * 256, :] = onehot(chosen & (place // 16 == g))

    def halves(ref):
        parts = [ref[:, h].astype(F32).reshape(rows, 128) for h in (0, 1)]
        return jnp.concatenate(parts, axis=1)

    load_hist.wait()
    past = [hist_v[:, h].astype(F32).reshape(hist_cols, 128) for h in (0, 1)]
    past = dot(kh[...], jnp.concatenate(past, axis=1).astype(BF16))

    chunk = rows // GROUPS

    def halo_copies(n):
        copies = [
            ((0, -1), edge_s.at[n, 0], below.at[n], 1),
            ((0, 1), edge_s.at[n, 1], above.at[n], 0),
        ]
        for dc in (-1, 1):
            side = 0 if dc == 1 else 1
            for dr in (-1, 0, 1):
                copies.append(
                    (
                        (dc, dr),
                        strip_s.at[n, side],
                        strips.at[n, 1 - dr, :, pl.ds(side * 128, 128)],
                        2 + side * 3 + 1 - dr,
                    )
                )
        return [
            (
                where,
                pltpu.make_async_remote_copy(
                    src_ref=source,
                    dst_ref=target,
                    send_sem=halo_send.at[n, slot],
                    recv_sem=halo_recv.at[n, slot],
                    device_id={"frames": col + where[0], "rows": row + where[1]},
                    device_id_type=MESH,
                ),
            )
            for where, source, target, slot in copies
        ]

    def halo_start(n, field):
        edge_s[n, 0] = field[:, 0:128]
        edge_s[n, 1] = field[:, 128:256]
        wide = [field[g * chunk : (g + 1) * chunk, :] for g in range(GROUPS)]
        packed = dot(jnp.concatenate(wide, axis=1), sel[...]).astype(BF16)
        strip_s[n, 0] = packed[:, 0:128]
        strip_s[n, 1] = packed[:, 128:256]
        for where, copy in halo_copies(n):

            @pl.when(exists[where])
            def _():
                copy.start()

    def halo_wait(n):
        for where, copy in halo_copies(n):

            @pl.when(exists[-where[0], -where[1]])
            def _():
                copy.wait_recv()

    def smooth(n, field):
        stacked = jnp.concatenate(
            [above[n], field[:, 0:128], field[:, 128:256], below[n]], axis=0
        )
        wide = dot(stacked, band[...])
        flat = wide[:, 0:128] + wide[:, 128:256]
        lines = strips[n].reshape(3 * chunk, 256)
        corner = dot(lines, hbh[...]) + dot(lines, hbl[...])

        def part(block, which, h):
            extra = [
                corner[which * chunk : (which + 1) * chunk, g * 256 + h * 128 : g * 256 + h * 128 + 128]
                for g in range(GROUPS)
            ]
            return flat[block * rows : (block + 1) * rows] + jnp.concatenate(extra, axis=0)

        blocks = [part(0, 0, 1), part(1, 1, 0), part(2, 1, 1), part(3, 2, 0)]
        pairs = [split(b) for b in blocks]
        result = []
        for q in range(rows // rg):
            cut = slice(q * rg, (q + 1) * rg)

            def tower(which):
                return jnp.concatenate(
                    [
                        jnp.concatenate([pairs[d][which][cut], pairs[d + 1][which][cut]], axis=1)
                        for d in range(3)
                    ],
                    axis=0,
                )

            high, low = tower(0), tower(1)
            result.append(dot(ah[...], high) + dot(ah[...], low) + dot(al[...], high))
        return jnp.concatenate(result, axis=0) * scale

    lane = iota((1, 128), 1)

    def reduce_over(it, stage, axis, count, me, value):
        row_s[it, stage] = value
        row_r[it, stage, pl.ds(me, 1)] = value.reshape(1, 1, 128)

        def send(k, carry):
            pltpu.make_async_remote_copy(
                src_ref=row_s.at[it, stage],
                dst_ref=row_r.at[it, stage, me],
                send_sem=sum_send.at[it, stage],
                recv_sem=sum_recv.at[it, stage],
                device_id={axis: lax.rem(me + k, count)},
                device_id_type=MESH,
            ).start()
            return carry

        lax.fori_loop(1, count, send, 0)
        wait_bytes(row_r.at[it, stage, pl.ds(0, count - 1)], sum_recv.at[it, stage])
        return jnp.sum(row_r[it, stage], axis=0)

    def step_size(it, norm, conv, curv):
        value = jnp.where(lane == 0, norm, jnp.where(lane == 1, conv, curv))
        value = reduce_over(it, 0, "frames", nf, col, value)
        value = reduce_over(it, 1, "rows", nr, row, value)
        return value[:, 0:1] / (value[:, 1:2] + REG_WEIGHT * value[:, 2:3])

    def total_of(value):
        return jnp.sum(value, keepdims=True)

    wait_bytes(hi_c, a2a_recv.at[0])
    point_bf = halves(hi_c).astype(BF16)
    halo_start(0, point_bf)
    seen = None
    steps = []
    for it in range(ITERS):
        now = dot(kw[...], point_bf)
        if it == 0:
            wait_bytes(obs_c, a2a_recv.at[1])
            past = past - halves(obs_c)
        resid_bf = (past + now).astype(BF16)
        back = dot(kwt[...], resid_bf).astype(BF16).astype(F32)
        halo_wait(2 * it)
        point_f = point_bf.astype(F32)
        gradient = back + REG_WEIGHT * (point_f - smooth(2 * it, point_bf))
        for h in (0, 1):
            grad_c[it, :, h] = gradient[:, h * 128 : (h + 1) * 128].reshape(frames, 8, 128)
        grad_bf = gradient.astype(BF16)
        halo_start(2 * it + 1, grad_bf)
        gradient_out(it)
        conv = dot(kw[...], grad_bf)
        norm, conv = total_of(gradient * gradient), total_of(conv * conv)
        halo_wait(2 * it + 1)
        grad_smooth = smooth(2 * it + 1, grad_bf)
        grad_f32 = grad_bf.astype(F32)
        curv = total_of(grad_f32 * (grad_f32 - grad_smooth))
        step = step_size(it, norm, conv, curv)
        steps.append(step)
        if it == 0:
            wait_bytes(lo_c, a2a_recv.at[2])
            point = halves(hi_c) + halves(lo_c)
            point = jnp.maximum(point - step * gradient - step * SPARSE_WEIGHT, 0.0)
            point_bf = point.astype(BF16)
            halo_start(2, point_bf)

    betas = momentum_terms(ITERS)
    for it in range(ITERS):
        wait_bytes(grad_f.at[it], a2a_recv.at[3 + it])
    for c in range(nf):
        cut = slice(c * 128, (c + 1) * 128)
        previous = start_f[:, :, :, cut]
        point = previous
        for it in range(ITERS):
            step = steps[it].reshape(1, 1, 1, 1)
            updated = jnp.maximum(
                point - step * grad_f[it, c] - step * SPARSE_WEIGHT, 0.0
            )
            point = updated + betas[it] * (updated - previous) if betas[it] else updated
            previous = updated
        out_spikes[:, :, :, cut] = previous
        out_point[:, :, :, cut] = point

    wait_bytes(hi_f.at[pl.ds(0, nf - 1)], a2a_send.at[0])
    wait_bytes(obs_c.at[pl.ds(0, per * (nf - 1))], a2a_send.at[1])
    wait_bytes(lo_f.at[pl.ds(0, nf - 1)], a2a_send.at[2])
    for it in range(ITERS):
        wait_bytes(grad_f.at[it, pl.ds(0, nf - 1)], a2a_send.at[3 + it])
        for stage, count in ((0, nf), (1, nr)):
            wait_bytes(row_r.at[it, stage, pl.ds(0, count - 1)], sum_send.at[it, stage])
        for n in (2 * it, 2 * it + 1):
            for where, copy in halo_copies(n):

                @pl.when(exists[where])
                def _():
                    copy.wait_send()


def shards(nf, nr, observed, history, spikes_start, kernel, smooth_half):
    per, _, tall, cols = observed.shape
    frames = per * nf
    rows = frames * 8
    hist = history.shape[0]
    assert tall == 16 and history.shape[3] == 128 and cols == 128 * nf
    hist_pad = hist + 1
    rg = min(rows, 256)
    chunk = rows // GROUPS
    most = max(nf, nr)
    block = (per, 2, 8, 128)
    any_spec = pl.BlockSpec(memory_space=pl.ANY)
    vmem = pl.BlockSpec(memory_space=pltpu.VMEM)
    out = jax.ShapeDtypeStruct((per, 2, 8, cols), F32)
    spikes, point = pl.pallas_call(
        functools.partial(body, nf, nr, frames),
        out_shape=(out, out),
        in_specs=[any_spec, any_spec, any_spec, vmem, pl.BlockSpec(memory_space=pltpu.SMEM)],
        out_specs=(vmem, vmem),
        scratch_shapes=[
            pltpu.VMEM((per, 2, 8, cols), F32),
            pltpu.VMEM((nf,) + block, BF16),
            pltpu.VMEM((nf,) + block, BF16),
            pltpu.VMEM((frames, 2, 8, 128), BF16),
            pltpu.VMEM((frames, 2, 8, 128), BF16),
            pltpu.VMEM((frames, 2, 8, 128), BF16),
            pltpu.VMEM((hist_pad, 2, 8, 128), BF16),
            pltpu.VMEM((ITERS, frames, 2, 8, 128), F32),
            pltpu.VMEM((ITERS, nf) + block, F32),
            pltpu.VMEM((2 * ITERS, 2, rows, 128), BF16),
            pltpu.VMEM((2 * ITERS, 2, chunk, 128), BF16),
            pltpu.VMEM((2 * ITERS, rows, 128), BF16),
            pltpu.VMEM((2 * ITERS, rows, 128), BF16),
            pltpu.VMEM((2 * ITERS, 3, chunk, 256), BF16),
            pltpu.VMEM((ITERS, 2, 1, 128), F32),
            pltpu.VMEM((ITERS, 2, most, 1, 128), F32),
            pltpu.VMEM((rows, 8 * hist_pad), BF16),
            pltpu.VMEM((rows, rows), BF16),
            pltpu.VMEM((rows, rows), BF16),
            pltpu.VMEM((128, 256), BF16),
            pltpu.VMEM((rg, 3 * rg), BF16),
            pltpu.VMEM((rg, 3 * rg), BF16),
            pltpu.VMEM((GROUPS * 256, 256), BF16),
            pltpu.VMEM((256, GROUPS * 256), BF16),
            pltpu.VMEM((256, GROUPS * 256), BF16),
            pltpu.SemaphoreType.DMA((2,)),
            pltpu.SemaphoreType.DMA((3 + ITERS,)),
            pltpu.SemaphoreType.DMA((3 + ITERS,)),
            pltpu.SemaphoreType.DMA((2 * ITERS, 8)),
            pltpu.SemaphoreType.DMA((2 * ITERS, 8)),
            pltpu.SemaphoreType.DMA((ITERS, 2)),
            pltpu.SemaphoreType.DMA((ITERS, 2)),
        ],
        compiler_params=pltpu.CompilerParams(
            collective_id=0, has_side_effects=True, vmem_limit_bytes=48 * 1024 * 1024
        ),
        name="fista",
    )(
        observed.reshape(per, 2, 8, cols),
        history.reshape(hist, 2, 8, 128),
        spikes_start.reshape(per, 2, 8, cols),
        kernel.reshape(1, -1),
        smooth_half,
    )
    shape = spikes_start.shape
    return spikes.reshape(shape), point.reshape(shape)


def solution(mesh):
    in_specs = (
        P("frames", None, "rows", None),
        P(None, None, "rows", "frames"),
        P("frames", None, "rows", None),
        P(),
        P(),
    )
    out_specs = (P("frames", None, "rows", None), P("frames", None, "rows", None))
    step = functools.partial(shards, mesh.shape["frames"], mesh.shape["rows"])
    return jax.shard_map(step, mesh=mesh, in_specs=in_specs, out_specs=out_specs, check_vma=False)
```

```python
import functools
import math

import jax
import jax.numpy as jnp
from jax import lax
from jax.experimental import pallas as pl
from jax.experimental.pallas import tpu as pltpu
from jax.sharding import PartitionSpec as P

ITERS = 2
REG_WEIGHT = 4.0
SPARSE_WEIGHT = 0.1
MESH = pl.DeviceIdType.MESH
F32 = jnp.float32
BF16 = jnp.bfloat16
GROUPS = 8


def momentum_terms(count):
    current = 1.0
    terms = []
    for iteration in range(count):
        upcoming = (1.0 + math.sqrt(1.0 + 4.0 * current * current)) / 2.0
        terms.append((current - 1.0) / upcoming)
        current = upcoming
    return terms


def iota(shape, dim):
    return lax.broadcasted_iota(jnp.int32, shape, dim)


def dot(a, b):
    return jnp.dot(a, b, preferred_element_type=F32)


def onehot(cond):
    return jnp.where(cond, 1.0, 0.0).astype(BF16)


def split(value):
    high = value.astype(BF16)
    return high, (value - high.astype(F32)).astype(BF16)


def body(
    nf,
    nr,
    frames,
    obs_hbm,
    hist_hbm,
    start_hbm,
    taps_hbm,
    half_hbm,
    out_first,
    out_slope,
    out_step,
    start_f,
    hi_f,
    lo_f,
    hi_c,
    lo_c,
    obs_c,
    hist_v,
    back_c,
    back_f,
    point_1,
    above_f,
    below_f,
    pull_f,
    first_f,
    slope_f,
    store_sems,
    taps_ref,
    half_ref,
    edge_s,
    strip_s,
    above,
    below,
    strips,
    row_s,
    row_r,
    kh,
    kw,
    kwt,
    band,
    ah,
    al,
    sel,
    hbh,
    hbl,
    local_sems,
    a2a_send,
    a2a_recv,
    halo_send,
    halo_recv,
    sum_send,
    sum_recv,
    wide_send,
    wide_recv,
):
    col = lax.axis_index("frames")
    row = lax.axis_index("rows")
    per = frames // nf
    rows = frames * 8
    hist_len = hist_hbm.shape[0]
    tap_count = taps_ref.shape[1]

    load_start = pltpu.make_async_copy(start_hbm, start_f, local_sems.at[0])
    load_start.start()
    load_hist = pltpu.make_async_copy(hist_hbm, hist_v.at[pl.ds(0, hist_len)], local_sems.at[1])
    load_hist.start()
    load_taps = pltpu.make_async_copy(taps_hbm, taps_ref, local_sems.at[2])
    load_taps.start()
    load_half = pltpu.make_async_copy(half_hbm, half_ref, local_sems.at[3])
    load_half.start()

    barrier = pltpu.get_barrier_semaphore()

    def signal_frames(k, carry):
        pl.semaphore_signal(
            barrier, inc=1, device_id={"frames": lax.rem(col + k, nf)}, device_id_type=MESH
        )
        return carry

    def signal_rows(k, carry):
        pl.semaphore_signal(
            barrier, inc=1, device_id={"rows": lax.rem(row + k, nr)}, device_id_type=MESH
        )
        return carry

    lax.fori_loop(1, nf, signal_frames, 0)
    lax.fori_loop(1, nr, signal_rows, 0)
    exists = {}
    for dc in (-1, 0, 1):
        for dr in (-1, 0, 1):
            conds = []
            if dc == -1:
                conds.append(col > 0)
            if dc == 1:
                conds.append(col < nf - 1)
            if dr == -1:
                conds.append(row > 0)
            if dr == 1:
                conds.append(row < nr - 1)
            if conds:
                exists[dc, dr] = functools.reduce(jnp.logical_and, conds)
    for dc in (-1, 1):
        for dr in (-1, 1):

            @pl.when(exists[dc, dr])
            def _():
                pl.semaphore_signal(
                    barrier,
                    inc=1,
                    device_id={"frames": col + dc, "rows": row + dr},
                    device_id_type=MESH,
                )

    load_start.wait()
    for c in range(nf):
        high, low = split(start_f[:, :, :, c * 128 : (c + 1) * 128])
        hi_f[c] = high
        lo_f[c] = low

    sides = (col > 0).astype(jnp.int32) + (col < nf - 1).astype(jnp.int32)
    ends = (row > 0).astype(jnp.int32) + (row < nr - 1).astype(jnp.int32)
    pl.semaphore_wait(barrier, (nf - 1) + (nr - 1) + sides * ends)

    def order(k):
        return nf // 2 + ((k + 1) // 2) * (1 - 2 * lax.rem(k, 2))

    def exchange(index, source, target, own_source, own_target):
        own = pltpu.make_async_copy(own_source, own_target, a2a_recv.at[index])
        own.start()

        def send(k, carry):
            peer = lax.rem(col + order(k), nf)
            pltpu.make_async_remote_copy(
                src_ref=source(peer),
                dst_ref=target,
                send_sem=a2a_send.at[index],
                recv_sem=a2a_recv.at[index],
                device_id={"frames": peer},
                device_id_type=MESH,
            ).start()
            return carry

        lax.fori_loop(0, nf - 1, send, 0)

    def wait_bytes(view, sem):
        pltpu.make_async_copy(view, view, sem).wait()

    def to_block(index, source, buffer):
        target = buffer.at[pl.ds(col * per, per)]
        exchange(index, source, target, source(col), target)

    to_block(0, lambda c: hi_f.at[c], hi_c)
    to_block(1, lambda c: obs_hbm.at[:, :, :, pl.ds(pl.multiple_of(c * 128, 128), 128)], obs_c)

    def back_out(it):
        target = back_f.at[it, col]
        exchange(
            3 + it,
            lambda f: back_c.at[it, pl.ds(f * per, per)],
            target,
            back_c.at[it, pl.ds(col * per, per)],
            target,
        )

    def wide_copies(it, buffer):
        copies = [((0, -1), 0, below_f), ((0, 1), 1, above_f)]
        return [
            (
                where,
                pltpu.make_async_remote_copy(
                    src_ref=buffer.at[:, :, h],
                    dst_ref=target.at[it],
                    send_sem=wide_send.at[it, h],
                    recv_sem=wide_recv.at[it, h],
                    device_id={"rows": row + where[1]},
                    device_id_type=MESH,
                ),
            )
            for where, h, target in copies
        ]

    def start_all(copies):
        for where, copy in copies:

            @pl.when(exists[where])
            def _():
                copy.start()

    def recv_all(copies):
        for where, copy in copies:

            @pl.when(exists[-where[0], -where[1]])
            def _():
                copy.wait_recv()

    def send_all(copies):
        for where, copy in copies:

            @pl.when(exists[where])
            def _():
                copy.wait_send()

    start_all(wide_copies(0, hi_f))

    def clear(ref):
        ref[...] = jnp.zeros(ref.shape, BF16)

    @pl.when(row == 0)
    def _():
        clear(above)
        clear(above_f)
        clear(strips.at[:, 0])

    @pl.when(row == nr - 1)
    def _():
        clear(below)
        clear(below_f)
        clear(strips.at[:, 2])

    @pl.when(col == 0)
    def _():
        clear(strips.at[:, :, :, pl.ds(0, 128)])

    @pl.when(col == nf - 1)
    def _():
        clear(strips.at[:, :, :, pl.ds(128, 128)])

    for n in range(1, 2 * ITERS, 2):
        clear(above.at[n, pl.ds(rows // 2, rows // 2)])
        clear(below.at[n, pl.ds(0, rows // 2)])

    hist_v[hist_len:] = jnp.zeros((hist_v.shape[0] - hist_len,) + hist_v.shape[1:], BF16)

    size = 256
    load_taps.wait()
    load_half.wait()
    spread = jnp.concatenate(
        [taps_ref[...].astype(F32), jnp.zeros((1, size - tap_count), F32)], axis=1
    )
    spread = jnp.broadcast_to(spread, (size, size))
    shifted = pltpu.roll(spread, size - (tap_count - 1), 1, stride=1, stride_axis=0).astype(BF16)
    at_t = onehot(iota((rows, size), 0) // 8 == iota((rows, size), 1))
    by_s = lax.dot_general(
        at_t, shifted, (((1,), (1,)), ((), ())), preferred_element_type=F32
    ).astype(BF16)

    def same_row(shape):
        return lax.rem(iota(shape, 0), 8) == lax.rem(iota(shape, 1), 8)

    hist_cols = kh.shape[1]
    s_of = iota((size, hist_cols), 0)
    pick = onehot((s_of == iota((size, hist_cols), 1) // 8) & (s_of < hist_len))
    kh[...] = jnp.where(same_row((rows, hist_cols)), dot(by_s, pick), 0.0).astype(BF16)
    pick = onehot(iota((size, rows), 0) == iota((size, rows), 1) // 8 + hist_len)
    kw[...] = jnp.where(same_row((rows, rows)), dot(by_s, pick), 0.0).astype(BF16)
    at_s = onehot(iota((rows, size), 0) // 8 + hist_len == iota((rows, size), 1))
    by_t = dot(at_s, shifted).astype(BF16)
    pick = onehot(iota((size, rows), 0) == iota((size, rows), 1) // 8)
    kwt[...] = jnp.where(same_row((rows, rows)), dot(by_t, pick), 0.0).astype(BF16)

    half = [half_ref[k] for k in range(half_ref.shape[0])]
    reach = half_ref.shape[0] - 1
    total = half[0]
    for k in range(1, reach + 1):
        total = total + 2.0 * half[k]
    total = jnp.full((1, 1), total, F32)
    scale = 1.0 / (total * total)

    def taps_at(distance):
        value = jnp.zeros(distance.shape, F32)
        for k in range(reach + 1):
            value = jnp.where(distance == k, half[k], value)
        return value

    high, low = split(taps_at(jnp.abs(iota((384, 128), 0) - 128 - iota((384, 128), 1))))
    band[:, 0:128] = high
    band[:, 128:256] = low

    rg = ah.shape[0]
    i0, i1 = iota((rg, rg), 0), iota((rg, rg), 1)
    for d in (-1, 0, 1):
        near = taps_at(jnp.abs(8 * d + lax.rem(i1, 8) - lax.rem(i0, 8)))
        high, low = split(jnp.where(i0 // 8 == i1 // 8, near, 0.0))
        ah[:, (d + 1) * rg : (d + 2) * rg] = high
        al[:, (d + 1) * rg : (d + 2) * rg] = low

    k0, k1 = iota((256, 256), 0), iota((256, 256), 1)
    place = lax.rem(k0, 128)
    inner, line = lax.rem(place, 8), lax.rem(k1, 128)
    near = taps_at(jnp.where(k0 < 128, line + 8 - inner, 128 + inner - line))
    near = jnp.where(lax.rem(place // 8, 2) == k1 // 128, near, 0.0)
    for g in range(GROUPS):
        high, low = split(jnp.where(place // 16 == g, near, 0.0))
        hbh[:, g * 256 : (g + 1) * 256] = high
        hbl[:, g * 256 : (g + 1) * 256] = low
    place = lax.rem(k1, 128)
    inner, line = lax.rem(place, 8), lax.rem(k0, 128)
    chosen = (lax.rem(place // 8, 2) == k0 // 128) & (line == jnp.where(k1 < 128, 120 + inner, inner))
    for g in range(GROUPS):
        sel[g * 256 : (g + 1) * 256, :] = onehot(chosen & (place // 16 == g))

    def halves(ref):
        parts = [ref[:, h].astype(F32).reshape(rows, 128) for h in (0, 1)]
        return jnp.concatenate(parts, axis=1)

    load_hist.wait()
    past = [hist_v[:, h].astype(F32).reshape(hist_cols, 128) for h in (0, 1)]
    past = dot(kh[...], jnp.concatenate(past, axis=1).astype(BF16))

    chunk = rows // GROUPS

    def edge_rows(n):
        cut = rows // 2 if n % 2 else rows
        return pl.ds(0, cut), pl.ds(rows - cut, cut)

    def halo_copies(n):
        upper, lower = edge_rows(n)
        copies = [
            ((0, -1), edge_s.at[n, 0, lower], below.at[n, lower], 1),
            ((0, 1), edge_s.at[n, 1, upper], above.at[n, upper], 0),
        ]
        for dc in (-1, 1):
            side = 0 if dc == 1 else 1
            for dr in (-1, 0, 1):
                copies.append(
                    (
                        (dc, dr),
                        strip_s.at[n, side],
                        strips.at[n, 1 - dr, :, pl.ds(side * 128, 128)],
                        2 + side * 3 + 1 - dr,
                    )
                )
        return [
            (
                where,
                pltpu.make_async_remote_copy(
                    src_ref=source,
                    dst_ref=target,
                    send_sem=halo_send.at[n, slot],
                    recv_sem=halo_recv.at[n, slot],
                    device_id={"frames": col + where[0], "rows": row + where[1]},
                    device_id_type=MESH,
                ),
            )
            for where, source, target, slot in copies
        ]

    def halo_start(n, field):
        upper, lower = edge_rows(n)
        weight = jnp.asarray(2.0 if n % 2 else 1.0, BF16)
        edge_s[n, 0, lower] = field[rows - lower.size :, 0:128] * weight
        edge_s[n, 1, upper] = field[: upper.size, 128:256] * weight
        wide = [field[g * chunk : (g + 1) * chunk, :] for g in range(GROUPS)]
        packed = dot(jnp.concatenate(wide, axis=1), sel[...]).astype(BF16)
        strip_s[n, 0] = packed[:, 0:128]
        strip_s[n, 1] = packed[:, 128:256]
        start_all(halo_copies(n))

    def smooth(n, field):
        stacked = jnp.concatenate(
            [above[n], field[:, 0:128], field[:, 128:256], below[n]], axis=0
        )
        wide = dot(stacked, band[128:256])
        flat = wide[:, 0:128] + wide[:, 128:256]
        lines = strips[n].reshape(3 * chunk, 256)
        corner = dot(lines, hbh[...]) + dot(lines, hbl[...])

        def part(block, which, h):
            extra = [
                corner[which * chunk : (which + 1) * chunk, g * 256 + h * 128 : g * 256 + h * 128 + 128]
                for g in range(GROUPS)
            ]
            if n % 2 and which != 1:
                gone = jnp.zeros((chunk, 128), F32)
                kept = (0, 1, 2, 3) if which == 0 else (4, 5, 6, 7)
                extra = [2.0 * extra[g] if g in kept else gone for g in range(GROUPS)]
            return flat[block * rows : (block + 1) * rows] + jnp.concatenate(extra, axis=0)

        return along_rows([part(0, 0, 1), part(1, 1, 0), part(2, 1, 1), part(3, 2, 0)])

    def smooth_wide(it, buffer):
        blocks = [above_f[it], buffer[:, :, 0], buffer[:, :, 1], below_f[it]]
        blocks = [b.astype(F32).reshape(rows, 128).astype(BF16) for b in blocks]
        step = 8 * per
        gap = jnp.zeros((step, 128), BF16)
        stacked = jnp.concatenate(
            [
                jnp.concatenate(
                    [
                        jnp.concatenate([gap, b[: rows - step]], axis=0),
                        b,
                        jnp.concatenate([b[step:], gap], axis=0),
                    ],
                    axis=1,
                )
                for b in blocks
            ],
            axis=0,
        )
        wide = dot(stacked, band[...])
        flat = wide[:, 0:128] + wide[:, 128:256]
        field = jnp.concatenate(blocks[1:3], axis=1).astype(F32)
        blocks = [flat[b * rows : (b + 1) * rows] for b in range(4)]
        pull_f[it] = REG_WEIGHT * (field - along_rows(blocks))

    def along_rows(blocks):
        pairs = [split(b) for b in blocks]
        result = []
        for q in range(rows // rg):
            cut = slice(q * rg, (q + 1) * rg)

            def tower(which):
                return jnp.concatenate(
                    [
                        jnp.concatenate([pairs[d][which][cut], pairs[d + 1][which][cut]], axis=1)
                        for d in range(3)
                    ],
                    axis=0,
                )

            high, low = tower(0), tower(1)
            result.append(dot(ah[...], high) + dot(ah[...], low) + dot(al[...], high))
        return jnp.concatenate(result, axis=0) * scale

    lane = iota((1, 128), 1)

    def sum_start(it, stage, value):
        axis, me, count = (("rows", row, nr), ("frames", col, nf))[stage]
        row_s[it, stage] = value
        row_r[it, stage, pl.ds(me, 1)] = value.reshape(1, 1, 128)

        def send(k, carry):
            pltpu.make_async_remote_copy(
                src_ref=row_s.at[it, stage],
                dst_ref=row_r.at[it, stage, me],
                send_sem=sum_send.at[it, stage],
                recv_sem=sum_recv.at[it, stage],
                device_id={axis: lax.rem(me + k, count)},
                device_id_type=MESH,
            ).start()
            return carry

        lax.fori_loop(1, count, send, 0)

    def sum_end(it, stage):
        count = (nr, nf)[stage]
        wait_bytes(row_r.at[it, stage, pl.ds(0, count - 1)], sum_recv.at[it, stage])
        return jnp.sum(row_r[it, stage], axis=0)

    def total_of(value):
        return jnp.sum(value, keepdims=True)

    recv_all(wide_copies(0, hi_f))
    smooth_wide(0, hi_f)

    def descend(point, pull, back, step):
        return jnp.maximum(point - step * (back + pull) - step * SPARSE_WEIGHT, 0.0)

    def wide_parts(c, h):
        cut = slice(c * 8 * per, (c + 1) * 8 * per)
        return cut, slice(h * 128, (h + 1) * 128)

    def update_first(step):
        wait_bytes(back_f.at[0], a2a_recv.at[3])
        for c in range(nf):
            for h in (0, 1):
                cut, lanes = wide_parts(c, h)
                where = slice(c * 128, (c + 1) * 128)
                point = start_f[:, h, :, where].reshape(8 * per, 128)
                back = back_f[0, c, :, h].astype(F32).reshape(8 * per, 128)
                updated = descend(point, pull_f[0, cut, lanes], back, step).reshape(per, 8, 128)
                first_f[:, h, :, where] = updated
                point_1[c, :, h] = updated.astype(BF16)
        start_all(wide_copies(1, point_1))
        store = pltpu.make_async_copy(first_f, out_first, store_sems.at[0])
        store.start()
        return store

    def slope_last():
        wait_bytes(back_f.at[1], a2a_recv.at[4])
        for c in range(nf):
            for h in (0, 1):
                cut, lanes = wide_parts(c, h)
                back = back_f[1, c, :, h].astype(F32).reshape(8 * per, 128)
                slope = (back + pull_f[1, cut, lanes]).reshape(per, 8, 128)
                slope_f[:, h, :, c * 128 : (c + 1) * 128] = slope
        store = pltpu.make_async_copy(slope_f, out_slope, store_sems.at[1])
        store.start()
        return store

    steps = []
    wait_bytes(hi_c, a2a_recv.at[0])
    point_bf = halves(hi_c).astype(BF16)
    halo_start(0, point_bf)
    for it in range(ITERS):
        now = dot(kw[...], point_bf)
        if it == 0:
            wait_bytes(obs_c, a2a_recv.at[1])
            past = past - halves(obs_c)
        resid_bf = (past + now).astype(BF16)
        back = dot(kwt[...], resid_bf)
        for h in (0, 1):
            part = back[:, h * 128 : (h + 1) * 128].reshape(frames, 8, 128)
            back_c[it, :, h] = part.astype(BF16)
        back = back.astype(BF16).astype(F32)
        recv_all(halo_copies(2 * it))
        point_f = point_bf.astype(F32)
        gradient = back + REG_WEIGHT * (point_f - smooth(2 * it, point_bf))
        grad_bf = gradient.astype(BF16)
        halo_start(2 * it + 1, grad_bf)
        if it == 0:
            to_block(2, lambda c: lo_f.at[c], lo_c)
        else:
            back_out(1)
        conv = dot(kw[...], grad_bf)
        norm, conv = total_of(gradient * gradient), total_of(conv * conv)
        if it == 1:
            store_first = update_first(steps[0])
        recv_all(halo_copies(2 * it + 1))
        grad_smooth = smooth(2 * it + 1, grad_bf)
        grad_f32 = grad_bf.astype(F32)
        curv = total_of(grad_f32 * (grad_f32 - grad_smooth))
        sum_start(it, 0, jnp.where(lane == 0, norm, jnp.where(lane == 1, conv, curv)))
        if it == 1:
            recv_all(wide_copies(1, point_1))
            smooth_wide(1, point_1)
        value = sum_end(it, 0)
        sum_start(it, 1, value)
        if it == 0:
            back_out(0)
        else:
            store_slope = slope_last()
        value = sum_end(it, 1)
        step = value[:, 0:1] / (value[:, 1:2] + REG_WEIGHT * value[:, 2:3])
        steps.append(step)
        if it == 0:
            wait_bytes(lo_c, a2a_recv.at[2])
            point = halves(hi_c) + halves(lo_c)
            point = jnp.maximum(point - step * gradient - step * SPARSE_WEIGHT, 0.0)
            point_bf = point.astype(BF16)
            halo_start(2, point_bf)
    out_step[...] = jnp.broadcast_to(step, out_step.shape)
    store_first.wait()
    store_slope.wait()

    wait_bytes(hi_f.at[pl.ds(0, nf - 1)], a2a_send.at[0])
    wait_bytes(obs_c.at[pl.ds(0, per * (nf - 1))], a2a_send.at[1])
    wait_bytes(lo_f.at[pl.ds(0, nf - 1)], a2a_send.at[2])
    for it in range(ITERS):
        wait_bytes(back_f.at[it, pl.ds(0, nf - 1)], a2a_send.at[3 + it])
        for stage, count in ((0, nr), (1, nf)):
            wait_bytes(row_r.at[it, stage, pl.ds(0, count - 1)], sum_send.at[it, stage])
        send_all(wide_copies(it, hi_f if it == 0 else point_1))
        for n in (2 * it, 2 * it + 1):
            send_all(halo_copies(n))


def shards(nf, nr, observed, history, spikes_start, kernel, smooth_half):
    per, _, tall, cols = observed.shape
    frames = per * nf
    rows = frames * 8
    hist = history.shape[0]
    assert tall == 16 and history.shape[3] == 128 and cols == 128 * nf
    hist_pad = hist + 1
    rg = min(rows, 256)
    chunk = rows // GROUPS
    most = max(nf, nr)
    block = (per, 2, 8, 128)
    any_spec = pl.BlockSpec(memory_space=pltpu.MemorySpace.HBM)
    vmem = pl.BlockSpec(memory_space=pltpu.VMEM)
    out = jax.ShapeDtypeStruct((per, 2, 8, cols), F32)
    first, slope, step = pl.pallas_call(
        functools.partial(body, nf, nr, frames),
        out_shape=(out, out, jax.ShapeDtypeStruct((1, 128), F32)),
        in_specs=[any_spec] * 5,
        out_specs=(any_spec, any_spec, vmem),
        scratch_shapes=[
            pltpu.VMEM((per, 2, 8, cols), F32),
            pltpu.VMEM((nf,) + block, BF16),
            pltpu.VMEM((nf,) + block, BF16),
            pltpu.VMEM((frames, 2, 8, 128), BF16),
            pltpu.VMEM((frames, 2, 8, 128), BF16),
            pltpu.VMEM((frames, 2, 8, 128), BF16),
            pltpu.VMEM((hist_pad, 2, 8, 128), BF16),
            pltpu.VMEM((ITERS, frames, 2, 8, 128), BF16),
            pltpu.VMEM((ITERS, nf) + block, BF16),
            pltpu.VMEM((nf,) + block, BF16),
            pltpu.VMEM((ITERS, nf, per, 8, 128), BF16),
            pltpu.VMEM((ITERS, nf, per, 8, 128), BF16),
            pltpu.VMEM((ITERS, rows, 256), F32),
            pltpu.VMEM((per, 2, 8, cols), F32),
            pltpu.VMEM((per, 2, 8, cols), F32),
            pltpu.SemaphoreType.DMA((2,)),
            pltpu.VMEM((1, kernel.shape[0]), BF16),
            pltpu.SMEM(smooth_half.shape, F32),
            pltpu.VMEM((2 * ITERS, 2, rows, 128), BF16),
            pltpu.VMEM((2 * ITERS, 2, chunk, 128), BF16),
            pltpu.VMEM((2 * ITERS, rows, 128), BF16),
            pltpu.VMEM((2 * ITERS, rows, 128), BF16),
            pltpu.VMEM((2 * ITERS, 3, chunk, 256), BF16),
            pltpu.VMEM((ITERS, 2, 1, 128), F32),
            pltpu.VMEM((ITERS, 2, most, 1, 128), F32),
            pltpu.VMEM((rows, 8 * hist_pad), BF16),
            pltpu.VMEM((rows, rows), BF16),
            pltpu.VMEM((rows, rows), BF16),
            pltpu.VMEM((384, 256), BF16),
            pltpu.VMEM((rg, 3 * rg), BF16),
            pltpu.VMEM((rg, 3 * rg), BF16),
            pltpu.VMEM((GROUPS * 256, 256), BF16),
            pltpu.VMEM((256, GROUPS * 256), BF16),
            pltpu.VMEM((256, GROUPS * 256), BF16),
            pltpu.SemaphoreType.DMA((4,)),
            pltpu.SemaphoreType.DMA((3 + ITERS,)),
            pltpu.SemaphoreType.DMA((3 + ITERS,)),
            pltpu.SemaphoreType.DMA((2 * ITERS, 8)),
            pltpu.SemaphoreType.DMA((2 * ITERS, 8)),
            pltpu.SemaphoreType.DMA((ITERS, 2)),
            pltpu.SemaphoreType.DMA((ITERS, 2)),
            pltpu.SemaphoreType.DMA((ITERS, 2)),
            pltpu.SemaphoreType.DMA((ITERS, 2)),
        ],
        compiler_params=pltpu.CompilerParams(
            collective_id=0, has_side_effects=True, vmem_limit_bytes=67043328
        ),
        name="fista",
    )(
        observed.reshape(per, 2, 8, cols),
        history.reshape(hist, 2, 8, 128),
        spikes_start.reshape(per, 2, 8, cols),
        kernel.reshape(1, -1),
        smooth_half,
    )
    shape = spikes_start.shape
    step = step[0, 0]
    beta = momentum_terms(ITERS)[-1]
    first, slope = first.reshape(shape), slope.reshape(shape)
    spikes = jnp.maximum(first - step * slope - step * SPARSE_WEIGHT, 0.0)
    return spikes, spikes + beta * (spikes - first)


def solution(mesh):
    in_specs = (
        P("frames", None, "rows", None),
        P(None, None, "rows", "frames"),
        P("frames", None, "rows", None),
        P(),
        P(),
    )
    out_specs = (P("frames", None, "rows", None), P("frames", None, "rows", None))
    step = functools.partial(shards, mesh.shape["frames"], mesh.shape["rows"])
    return jax.shard_map(step, mesh=mesh, in_specs=in_specs, out_specs=out_specs, check_vma=False)
```

```python
import functools
import math

import jax
import jax.numpy as jnp
from jax import lax
from jax.experimental import pallas as pl
from jax.experimental.pallas import tpu as pltpu
from jax.sharding import PartitionSpec as P

ITERS = 2
REG_WEIGHT = 4.0
SPARSE_WEIGHT = 0.1
MESH = pl.DeviceIdType.MESH
F32 = jnp.float32
BF16 = jnp.bfloat16
GROUPS = 8
HALOS = 6
CURVATURE = (1, 3)


def momentum_terms(count):
    current = 1.0
    terms = []
    for iteration in range(count):
        upcoming = (1.0 + math.sqrt(1.0 + 4.0 * current * current)) / 2.0
        terms.append((current - 1.0) / upcoming)
        current = upcoming
    return terms


def iota(shape, dim):
    return lax.broadcasted_iota(jnp.int32, shape, dim)


def dot(a, b):
    return jnp.dot(a, b, preferred_element_type=F32)


def onehot(cond):
    return jnp.where(cond, 1.0, 0.0).astype(BF16)


def split(value):
    high = value.astype(BF16)
    return high, (value - high.astype(F32)).astype(BF16)


def body(
    nf,
    nr,
    frames,
    obs_hbm,
    hist_hbm,
    start_hbm,
    taps_hbm,
    half_hbm,
    out_first,
    out_slope,
    out_step,
    start_f,
    hi_f,
    lo_f,
    hi_c,
    lo_c,
    obs_c,
    hist_v,
    back_c,
    back_f,
    point_1,
    above_f,
    below_f,
    pull_f,
    first_f,
    slope_f,
    store_sems,
    taps_ref,
    half_ref,
    edge_s,
    strip_s,
    above,
    below,
    strips,
    row_s,
    row_r,
    kh,
    kw,
    kwt,
    band,
    ah,
    al,
    sel,
    hbh,
    hbl,
    local_sems,
    a2a_send,
    a2a_recv,
    halo_send,
    halo_recv,
    sum_send,
    sum_recv,
    wide_send,
    wide_recv,
):
    col = lax.axis_index("frames")
    row = lax.axis_index("rows")
    per = frames // nf
    rows = frames * 8
    hist_len = hist_hbm.shape[0]
    tap_count = taps_ref.shape[1]

    load_start = pltpu.make_async_copy(start_hbm, start_f, local_sems.at[0])
    load_start.start()
    load_hist = pltpu.make_async_copy(hist_hbm, hist_v.at[pl.ds(0, hist_len)], local_sems.at[1])
    load_hist.start()
    load_taps = pltpu.make_async_copy(taps_hbm, taps_ref, local_sems.at[2])
    load_taps.start()
    load_half = pltpu.make_async_copy(half_hbm, half_ref, local_sems.at[3])
    load_half.start()

    barrier = pltpu.get_barrier_semaphore()

    def signal_frames(k, carry):
        pl.semaphore_signal(
            barrier, inc=1, device_id={"frames": lax.rem(col + k, nf)}, device_id_type=MESH
        )
        return carry

    def signal_rows(k, carry):
        pl.semaphore_signal(
            barrier, inc=1, device_id={"rows": lax.rem(row + k, nr)}, device_id_type=MESH
        )
        return carry

    lax.fori_loop(1, nf, signal_frames, 0)
    lax.fori_loop(1, nr, signal_rows, 0)
    exists = {}
    for dc in (-1, 0, 1):
        for dr in (-1, 0, 1):
            conds = []
            if dc == -1:
                conds.append(col > 0)
            if dc == 1:
                conds.append(col < nf - 1)
            if dr == -1:
                conds.append(row > 0)
            if dr == 1:
                conds.append(row < nr - 1)
            if conds:
                exists[dc, dr] = functools.reduce(jnp.logical_and, conds)
    for dc in (-1, 1):
        for dr in (-1, 1):

            @pl.when(exists[dc, dr])
            def _():
                pl.semaphore_signal(
                    barrier,
                    inc=1,
                    device_id={"frames": col + dc, "rows": row + dr},
                    device_id_type=MESH,
                )

    load_start.wait()
    for c in range(nf):
        high, low = split(start_f[:, :, :, c * 128 : (c + 1) * 128])
        hi_f[c] = high
        lo_f[c] = low

    sides = (col > 0).astype(jnp.int32) + (col < nf - 1).astype(jnp.int32)
    ends = (row > 0).astype(jnp.int32) + (row < nr - 1).astype(jnp.int32)
    pl.semaphore_wait(barrier, (nf - 1) + (nr - 1) + sides * ends)

    def order(k):
        return nf // 2 + ((k + 1) // 2) * (1 - 2 * lax.rem(k, 2))

    def exchange(index, source, target, own_source, own_target):
        own = pltpu.make_async_copy(own_source, own_target, a2a_recv.at[index])
        own.start()

        def send(k, carry):
            peer = lax.rem(col + order(k), nf)
            pltpu.make_async_remote_copy(
                src_ref=source(peer),
                dst_ref=target,
                send_sem=a2a_send.at[index],
                recv_sem=a2a_recv.at[index],
                device_id={"frames": peer},
                device_id_type=MESH,
            ).start()
            return carry

        lax.fori_loop(0, nf - 1, send, 0)

    def wait_bytes(view, sem):
        pltpu.make_async_copy(view, view, sem).wait()

    def to_block(index, source, buffer):
        target = buffer.at[pl.ds(col * per, per)]
        exchange(index, source, target, source(col), target)

    to_block(0, lambda c: hi_f.at[c], hi_c)
    to_block(1, lambda c: obs_hbm.at[:, :, :, pl.ds(pl.multiple_of(c * 128, 128), 128)], obs_c)

    def back_out(it):
        target = back_f.at[it, col]
        exchange(
            3 + it,
            lambda f: back_c.at[it, pl.ds(f * per, per)],
            target,
            back_c.at[it, pl.ds(col * per, per)],
            target,
        )

    def wide_copies(it, buffer):
        copies = [((0, -1), 0, below_f), ((0, 1), 1, above_f)]
        return [
            (
                where,
                pltpu.make_async_remote_copy(
                    src_ref=buffer.at[:, :, h],
                    dst_ref=target.at[it],
                    send_sem=wide_send.at[it, h],
                    recv_sem=wide_recv.at[it, h],
                    device_id={"rows": row + where[1]},
                    device_id_type=MESH,
                ),
            )
            for where, h, target in copies
        ]

    def start_all(copies):
        for where, copy in copies:

            @pl.when(exists[where])
            def _():
                copy.start()

    def recv_all(copies):
        for where, copy in copies:

            @pl.when(exists[-where[0], -where[1]])
            def _():
                copy.wait_recv()

    def send_all(copies):
        for where, copy in copies:

            @pl.when(exists[where])
            def _():
                copy.wait_send()

    start_all(wide_copies(0, hi_f))

    def clear(ref):
        ref[...] = jnp.zeros(ref.shape, BF16)

    @pl.when(row == 0)
    def _():
        clear(above)
        clear(above_f)
        clear(strips.at[:, 0])

    @pl.when(row == nr - 1)
    def _():
        clear(below)
        clear(below_f)
        clear(strips.at[:, 2])

    @pl.when(col == 0)
    def _():
        clear(strips.at[:, :, :, pl.ds(0, 128)])

    @pl.when(col == nf - 1)
    def _():
        clear(strips.at[:, :, :, pl.ds(128, 128)])

    hist_v[hist_len:] = jnp.zeros((hist_v.shape[0] - hist_len,) + hist_v.shape[1:], BF16)

    size = 256
    load_taps.wait()
    load_half.wait()
    spread = jnp.concatenate(
        [taps_ref[...].astype(F32), jnp.zeros((1, size - tap_count), F32)], axis=1
    )
    spread = jnp.broadcast_to(spread, (size, size))
    shifted = pltpu.roll(spread, size - (tap_count - 1), 1, stride=1, stride_axis=0).astype(BF16)
    at_t = onehot(iota((rows, size), 0) // 8 == iota((rows, size), 1))
    by_s = lax.dot_general(
        at_t, shifted, (((1,), (1,)), ((), ())), preferred_element_type=F32
    ).astype(BF16)

    def same_row(shape):
        return lax.rem(iota(shape, 0), 8) == lax.rem(iota(shape, 1), 8)

    hist_cols = kh.shape[1]
    s_of = iota((size, hist_cols), 0)
    pick = onehot((s_of == iota((size, hist_cols), 1) // 8) & (s_of < hist_len))
    kh[...] = jnp.where(same_row((rows, hist_cols)), dot(by_s, pick), 0.0).astype(BF16)
    pick = onehot(iota((size, rows), 0) == iota((size, rows), 1) // 8 + hist_len)
    kw[...] = jnp.where(same_row((rows, rows)), dot(by_s, pick), 0.0).astype(BF16)
    at_s = onehot(iota((rows, size), 0) // 8 + hist_len == iota((rows, size), 1))
    by_t = dot(at_s, shifted).astype(BF16)
    pick = onehot(iota((size, rows), 0) == iota((size, rows), 1) // 8)
    kwt[...] = jnp.where(same_row((rows, rows)), dot(by_t, pick), 0.0).astype(BF16)

    half = [half_ref[k] for k in range(half_ref.shape[0])]
    reach = half_ref.shape[0] - 1
    total = half[0]
    for k in range(1, reach + 1):
        total = total + 2.0 * half[k]
    total = jnp.full((1, 1), total, F32)
    scale = 1.0 / (total * total)

    def taps_at(distance):
        value = jnp.zeros(distance.shape, F32)
        for k in range(reach + 1):
            value = jnp.where(distance == k, half[k], value)
        return value

    high, low = split(taps_at(jnp.abs(iota((384, 128), 0) - 128 - iota((384, 128), 1))))
    band[:, 0:128] = high
    band[:, 128:256] = low

    rg = ah.shape[0]
    i0, i1 = iota((rg, rg), 0), iota((rg, rg), 1)
    for d in (-1, 0, 1):
        near = taps_at(jnp.abs(8 * d + lax.rem(i1, 8) - lax.rem(i0, 8)))
        high, low = split(jnp.where(i0 // 8 == i1 // 8, near, 0.0))
        ah[:, (d + 1) * rg : (d + 2) * rg] = high
        al[:, (d + 1) * rg : (d + 2) * rg] = low

    k0, k1 = iota((256, 256), 0), iota((256, 256), 1)
    place = lax.rem(k0, 128)
    inner, line = lax.rem(place, 8), lax.rem(k1, 128)
    near = taps_at(jnp.where(k0 < 128, line + 8 - inner, 128 + inner - line))
    near = jnp.where(lax.rem(place // 8, 2) == k1 // 128, near, 0.0)
    for g in range(GROUPS):
        high, low = split(jnp.where(place // 16 == g, near, 0.0))
        hbh[:, g * 256 : (g + 1) * 256] = high
        hbl[:, g * 256 : (g + 1) * 256] = low
    place = lax.rem(k1, 128)
    inner, line = lax.rem(place, 8), lax.rem(k0, 128)
    chosen = (lax.rem(place // 8, 2) == k0 // 128) & (line == jnp.where(k1 < 128, 120 + inner, inner))
    for g in range(GROUPS):
        sel[g * 256 : (g + 1) * 256, :] = onehot(chosen & (place // 16 == g))

    def halves(ref):
        parts = [ref[:, h].astype(F32).reshape(rows, 128) for h in (0, 1)]
        return jnp.concatenate(parts, axis=1)

    load_hist.wait()
    past = [hist_v[:, h].astype(F32).reshape(hist_cols, 128) for h in (0, 1)]
    past = dot(kh[...], jnp.concatenate(past, axis=1).astype(BF16))

    chunk = rows // GROUPS

    def edge_rows(n):
        cut = rows // 2 if n in CURVATURE else rows
        return pl.ds(0, cut), pl.ds(rows - cut, cut)

    def edge_copy(n, dr, part, slot):
        source, target = (edge_s.at[n, 0], below) if dr == -1 else (edge_s.at[n, 1], above)
        return (
            (0, dr),
            pltpu.make_async_remote_copy(
                src_ref=source.at[part],
                dst_ref=target.at[n, part],
                send_sem=halo_send.at[n, slot],
                recv_sem=halo_recv.at[n, slot],
                device_id={"rows": row + dr},
                device_id_type=MESH,
            ),
        )

    def rest_copies(n):
        half_rows = rows // 2
        return [
            edge_copy(n, -1, pl.ds(0, half_rows), 8),
            edge_copy(n, 1, pl.ds(half_rows, half_rows), 9),
        ]

    def halo_copies(n):
        upper, lower = edge_rows(n)
        result = [edge_copy(n, -1, lower, 1), edge_copy(n, 1, upper, 0)]
        copies = []
        for dc in (-1, 1):
            side = 0 if dc == 1 else 1
            for dr in (-1, 0, 1):
                copies.append(
                    (
                        (dc, dr),
                        strip_s.at[n, side],
                        strips.at[n, 1 - dr, :, pl.ds(side * 128, 128)],
                        2 + side * 3 + 1 - dr,
                    )
                )
        return result + [
            (
                where,
                pltpu.make_async_remote_copy(
                    src_ref=source,
                    dst_ref=target,
                    send_sem=halo_send.at[n, slot],
                    recv_sem=halo_recv.at[n, slot],
                    device_id={"frames": col + where[0], "rows": row + where[1]},
                    device_id_type=MESH,
                ),
            )
            for where, source, target, slot in copies
        ]

    def halo_start(n, field):
        edge_s[n, 0] = field[:, 0:128]
        edge_s[n, 1] = field[:, 128:256]
        wide = [field[g * chunk : (g + 1) * chunk, :] for g in range(GROUPS)]
        packed = dot(jnp.concatenate(wide, axis=1), sel[...]).astype(BF16)
        strip_s[n, 0] = packed[:, 0:128]
        strip_s[n, 1] = packed[:, 128:256]
        start_all(halo_copies(n))

    def smooth(n, field):
        if n in CURVATURE:
            cut = rows // 2
            gone, twice = jnp.zeros((cut, 128), BF16), jnp.asarray(2.0, BF16)
            outer = [above[n, 0:cut] * twice, gone], [gone, below[n, cut:rows] * twice]
        else:
            outer = [above[n]], [below[n]]
        stacked = jnp.concatenate(
            [*outer[0], field[:, 0:128], field[:, 128:256], *outer[1]], axis=0
        )
        wide = dot(stacked, band[128:256])
        flat = wide[:, 0:128] + wide[:, 128:256]
        lines = strips[n].reshape(3 * chunk, 256)
        corner = dot(lines, hbh[...]) + dot(lines, hbl[...])

        def part(block, which, h):
            extra = [
                corner[which * chunk : (which + 1) * chunk, g * 256 + h * 128 : g * 256 + h * 128 + 128]
                for g in range(GROUPS)
            ]
            if n in CURVATURE and which != 1:
                gone = jnp.zeros((chunk, 128), F32)
                kept = (0, 1, 2, 3) if which == 0 else (4, 5, 6, 7)
                extra = [2.0 * extra[g] if g in kept else gone for g in range(GROUPS)]
            return flat[block * rows : (block + 1) * rows] + jnp.concatenate(extra, axis=0)

        return along_rows([part(0, 0, 1), part(1, 1, 0), part(2, 1, 1), part(3, 2, 0)])

    def smooth_wide(it, buffer):
        blocks = [above_f[it], buffer[:, :, 0], buffer[:, :, 1], below_f[it]]
        blocks = [b.astype(F32).reshape(rows, 128).astype(BF16) for b in blocks]
        step = 8 * per
        gap = jnp.zeros((step, 128), BF16)
        stacked = jnp.concatenate(
            [
                jnp.concatenate(
                    [
                        jnp.concatenate([gap, b[: rows - step]], axis=0),
                        b,
                        jnp.concatenate([b[step:], gap], axis=0),
                    ],
                    axis=1,
                )
                for b in blocks
            ],
            axis=0,
        )
        wide = dot(stacked, band[...])
        flat = wide[:, 0:128] + wide[:, 128:256]
        field = jnp.concatenate(blocks[1:3], axis=1).astype(F32)
        blocks = [flat[b * rows : (b + 1) * rows] for b in range(4)]
        pull_f[it] = REG_WEIGHT * (field - along_rows(blocks))

    def along_rows(blocks):
        pairs = [split(b) for b in blocks]
        result = []
        for q in range(rows // rg):
            cut = slice(q * rg, (q + 1) * rg)

            def tower(which):
                return jnp.concatenate(
                    [
                        jnp.concatenate([pairs[d][which][cut], pairs[d + 1][which][cut]], axis=1)
                        for d in range(3)
                    ],
                    axis=0,
                )

            high, low = tower(0), tower(1)
            result.append(dot(ah[...], high) + dot(ah[...], low) + dot(al[...], high))
        return jnp.concatenate(result, axis=0) * scale

    lane = iota((1, 128), 1)

    def sum_start(it, stage, value):
        axis, me, count = (("rows", row, nr), ("frames", col, nf))[stage]
        row_s[it, stage] = value
        row_r[it, stage, pl.ds(me, 1)] = value.reshape(1, 1, 128)

        def send(k, carry):
            pltpu.make_async_remote_copy(
                src_ref=row_s.at[it, stage],
                dst_ref=row_r.at[it, stage, me],
                send_sem=sum_send.at[it, stage],
                recv_sem=sum_recv.at[it, stage],
                device_id={axis: lax.rem(me + k, count)},
                device_id_type=MESH,
            ).start()
            return carry

        lax.fori_loop(1, count, send, 0)

    def sum_end(it, stage):
        count = (nr, nf)[stage]
        wait_bytes(row_r.at[it, stage, pl.ds(0, count - 1)], sum_recv.at[it, stage])
        return jnp.sum(row_r[it, stage], axis=0)

    def total_of(value):
        return jnp.sum(value, keepdims=True)

    recv_all(wide_copies(0, hi_f))
    smooth_wide(0, hi_f)

    def descend(point, pull, back, step):
        return jnp.maximum(point - step * (back + pull) - step * SPARSE_WEIGHT, 0.0)

    def wide_parts(c, h):
        cut = slice(c * 8 * per, (c + 1) * 8 * per)
        return cut, slice(h * 128, (h + 1) * 128)

    def update_first(step):
        wait_bytes(back_f.at[0], a2a_recv.at[3])
        for c in range(nf):
            for h in (0, 1):
                cut, lanes = wide_parts(c, h)
                where = slice(c * 128, (c + 1) * 128)
                point = start_f[:, h, :, where].reshape(8 * per, 128)
                back = back_f[0, c, :, h].astype(F32).reshape(8 * per, 128)
                updated = descend(point, pull_f[0, cut, lanes], back, step).reshape(per, 8, 128)
                first_f[:, h, :, where] = updated
                point_1[c, :, h] = updated.astype(BF16)
        start_all(wide_copies(1, point_1))
        store = pltpu.make_async_copy(first_f, out_first, store_sems.at[0])
        store.start()
        return store

    def slope_last():
        wait_bytes(back_f.at[1], a2a_recv.at[4])
        for c in range(nf):
            for h in (0, 1):
                cut, lanes = wide_parts(c, h)
                back = back_f[1, c, :, h].astype(F32).reshape(8 * per, 128)
                slope = (back + pull_f[1, cut, lanes]).reshape(per, 8, 128)
                slope_f[:, h, :, c * 128 : (c + 1) * 128] = slope
        store = pltpu.make_async_copy(slope_f, out_slope, store_sems.at[1])
        store.start()
        return store

    steps = []
    wait_bytes(hi_c, a2a_recv.at[0])
    point_bf = halves(hi_c).astype(BF16)
    halo_start(0, point_bf)
    to_block(2, lambda c: lo_f.at[c], lo_c)
    for it in range(ITERS):
        now = dot(kw[...], point_bf)
        if it == 0:
            wait_bytes(obs_c, a2a_recv.at[1])
            past = past - halves(obs_c)
        resid_bf = (past + now).astype(BF16)
        back = dot(kwt[...], resid_bf)
        for h in (0, 1):
            part = back[:, h * 128 : (h + 1) * 128].reshape(frames, 8, 128)
            back_c[it, :, h] = part.astype(BF16)
        back = back.astype(BF16).astype(F32)
        if it == 0:
            recv_all(halo_copies(0))
        point_f = point_bf.astype(F32)
        gradient = back + REG_WEIGHT * (point_f - smooth(2 * it, point_bf))
        grad_bf = gradient.astype(BF16)
        halo_start(2 * it + 1, grad_bf)
        back_out(it)
        if it == 0:
            start_all(rest_copies(1))
            halo_start(4, (gradient - grad_bf.astype(F32)).astype(BF16))
        conv = dot(kw[...], grad_bf)
        norm, conv = total_of(gradient * gradient), total_of(conv * conv)
        if it == 1:
            store_first = update_first(steps[0])
        recv_all(halo_copies(2 * it + 1))
        grad_smooth = smooth(2 * it + 1, grad_bf)
        grad_f32 = grad_bf.astype(F32)
        curv = total_of(grad_f32 * (grad_f32 - grad_smooth))
        sum_start(it, 0, jnp.where(lane == 0, norm, jnp.where(lane == 1, conv, curv)))
        if it == 0:
            wait_bytes(lo_c, a2a_recv.at[2])
            low = halves(lo_c)
            halo_start(5, low.astype(BF16))
        else:
            recv_all(wide_copies(1, point_1))
            smooth_wide(1, point_1)
        value = sum_end(it, 0)
        sum_start(it, 1, value)
        if it == 0:
            recv_all(rest_copies(1))
            recv_all(halo_copies(4))
            recv_all(halo_copies(5))
        else:
            store_slope = slope_last()
        value = sum_end(it, 1)
        step = value[:, 0:1] / (value[:, 1:2] + REG_WEIGHT * value[:, 2:3])
        steps.append(step)
        if it == 0:
            point = descend(halves(hi_c) + low, 0.0, gradient, step)
            point_bf = point.astype(BF16)
            for ref in (above, below, strips):
                start, slope = (
                    ref[high].astype(F32) + ref[low_part].astype(F32)
                    for high, low_part in ((0, 5), (1, 4))
                )
                ref[2] = descend(start, 0.0, slope, step).astype(BF16)
    out_step[...] = jnp.broadcast_to(step, out_step.shape)
    store_first.wait()
    store_slope.wait()

    wait_bytes(hi_f.at[pl.ds(0, nf - 1)], a2a_send.at[0])
    wait_bytes(obs_c.at[pl.ds(0, per * (nf - 1))], a2a_send.at[1])
    wait_bytes(lo_f.at[pl.ds(0, nf - 1)], a2a_send.at[2])
    for it in range(ITERS):
        wait_bytes(back_f.at[it, pl.ds(0, nf - 1)], a2a_send.at[3 + it])
        for stage, count in ((0, nr), (1, nf)):
            wait_bytes(row_r.at[it, stage, pl.ds(0, count - 1)], sum_send.at[it, stage])
        send_all(wide_copies(it, hi_f if it == 0 else point_1))
        for n in ((0, 1, 3), (4, 5))[it]:
            send_all(halo_copies(n))
    send_all(rest_copies(1))


def shards(nf, nr, observed, history, spikes_start, kernel, smooth_half):
    per, _, tall, cols = observed.shape
    frames = per * nf
    rows = frames * 8
    hist = history.shape[0]
    assert tall == 16 and history.shape[3] == 128 and cols == 128 * nf
    hist_pad = hist + 1
    rg = min(rows, 256)
    chunk = rows // GROUPS
    most = max(nf, nr)
    block = (per, 2, 8, 128)
    any_spec = pl.BlockSpec(memory_space=pltpu.MemorySpace.HBM)
    vmem = pl.BlockSpec(memory_space=pltpu.VMEM)
    out = jax.ShapeDtypeStruct((per, 2, 8, cols), F32)
    first, slope, step = pl.pallas_call(
        functools.partial(body, nf, nr, frames),
        out_shape=(out, out, jax.ShapeDtypeStruct((1, 128), F32)),
        in_specs=[any_spec] * 5,
        out_specs=(any_spec, any_spec, vmem),
        scratch_shapes=[
            pltpu.VMEM((per, 2, 8, cols), F32),
            pltpu.VMEM((nf,) + block, BF16),
            pltpu.VMEM((nf,) + block, BF16),
            pltpu.VMEM((frames, 2, 8, 128), BF16),
            pltpu.VMEM((frames, 2, 8, 128), BF16),
            pltpu.VMEM((frames, 2, 8, 128), BF16),
            pltpu.VMEM((hist_pad, 2, 8, 128), BF16),
            pltpu.VMEM((ITERS, frames, 2, 8, 128), BF16),
            pltpu.VMEM((ITERS, nf) + block, BF16),
            pltpu.VMEM((nf,) + block, BF16),
            pltpu.VMEM((ITERS, nf, per, 8, 128), BF16),
            pltpu.VMEM((ITERS, nf, per, 8, 128), BF16),
            pltpu.VMEM((ITERS, rows, 256), F32),
            pltpu.VMEM((per, 2, 8, cols), F32),
            pltpu.VMEM((per, 2, 8, cols), F32),
            pltpu.SemaphoreType.DMA((2,)),
            pltpu.VMEM((1, kernel.shape[0]), BF16),
            pltpu.SMEM(smooth_half.shape, F32),
            pltpu.VMEM((HALOS, 2, rows, 128), BF16),
            pltpu.VMEM((HALOS, 2, chunk, 128), BF16),
            pltpu.VMEM((HALOS, rows, 128), BF16),
            pltpu.VMEM((HALOS, rows, 128), BF16),
            pltpu.VMEM((HALOS, 3, chunk, 256), BF16),
            pltpu.VMEM((ITERS, 2, 1, 128), F32),
            pltpu.VMEM((ITERS, 2, most, 1, 128), F32),
            pltpu.VMEM((rows, 8 * hist_pad), BF16),
            pltpu.VMEM((rows, rows), BF16),
            pltpu.VMEM((rows, rows), BF16),
            pltpu.VMEM((384, 256), BF16),
            pltpu.VMEM((rg, 3 * rg), BF16),
            pltpu.VMEM((rg, 3 * rg), BF16),
            pltpu.VMEM((GROUPS * 256, 256), BF16),
            pltpu.VMEM((256, GROUPS * 256), BF16),
            pltpu.VMEM((256, GROUPS * 256), BF16),
            pltpu.SemaphoreType.DMA((4,)),
            pltpu.SemaphoreType.DMA((3 + ITERS,)),
            pltpu.SemaphoreType.DMA((3 + ITERS,)),
            pltpu.SemaphoreType.DMA((HALOS, 10)),
            pltpu.SemaphoreType.DMA((HALOS, 10)),
            pltpu.SemaphoreType.DMA((ITERS, 2)),
            pltpu.SemaphoreType.DMA((ITERS, 2)),
            pltpu.SemaphoreType.DMA((ITERS, 2)),
            pltpu.SemaphoreType.DMA((ITERS, 2)),
        ],
        compiler_params=pltpu.CompilerParams(
            collective_id=0, has_side_effects=True, vmem_limit_bytes=67043328
        ),
        name="fista",
    )(
        observed.reshape(per, 2, 8, cols),
        history.reshape(hist, 2, 8, 128),
        spikes_start.reshape(per, 2, 8, cols),
        kernel.reshape(1, -1),
        smooth_half,
    )
    shape = spikes_start.shape
    step = step[0, 0]
    beta = momentum_terms(ITERS)[-1]
    first, slope = first.reshape(shape), slope.reshape(shape)
    spikes = jnp.maximum(first - step * slope - step * SPARSE_WEIGHT, 0.0)
    return spikes, spikes + beta * (spikes - first)


def solution(mesh):
    in_specs = (
        P("frames", None, "rows", None),
        P(None, None, "rows", "frames"),
        P("frames", None, "rows", None),
        P(),
        P(),
    )
    out_specs = (P("frames", None, "rows", None), P("frames", None, "rows", None))
    step = functools.partial(shards, mesh.shape["frames"], mesh.shape["rows"])
    return jax.shard_map(step, mesh=mesh, in_specs=in_specs, out_specs=out_specs, check_vma=False)
```

```python
import functools
import math

import jax
import jax.numpy as jnp
from jax import lax
from jax.experimental import pallas as pl
from jax.experimental.pallas import tpu as pltpu
from jax.sharding import PartitionSpec as P

ITERS = 2
REG_WEIGHT = 4.0
SPARSE_WEIGHT = 0.1
MESH = pl.DeviceIdType.MESH
F32 = jnp.float32
BF16 = jnp.bfloat16
GROUPS = 8
HALOS = 6
CURVATURE = (1, 3)


def momentum_terms(count):
    current = 1.0
    terms = []
    for iteration in range(count):
        upcoming = (1.0 + math.sqrt(1.0 + 4.0 * current * current)) / 2.0
        terms.append((current - 1.0) / upcoming)
        current = upcoming
    return terms


def iota(shape, dim):
    return lax.broadcasted_iota(jnp.int32, shape, dim)


def dot(a, b):
    return jnp.dot(a, b, preferred_element_type=F32)


def onehot(cond):
    return jnp.where(cond, 1.0, 0.0).astype(BF16)


def split(value):
    high = value.astype(BF16)
    return high, (value - high.astype(F32)).astype(BF16)


def body(
    nf,
    nr,
    frames,
    obs_hbm,
    hist_hbm,
    start_hbm,
    taps_hbm,
    half_hbm,
    out_first,
    out_slope,
    out_step,
    start_f,
    hi_f,
    lo_f,
    hi_c,
    lo_c,
    obs_c,
    hist_v,
    back_c,
    back_f,
    point_1,
    above_f,
    below_f,
    pull_f,
    first_f,
    slope_f,
    store_sems,
    taps_ref,
    half_ref,
    edge_s,
    strip_s,
    above,
    below,
    strips,
    row_s,
    row_r,
    kh,
    kw,
    kwt,
    band,
    ah,
    al,
    sel,
    hbh,
    hbl,
    local_sems,
    a2a_send,
    a2a_recv,
    halo_send,
    halo_recv,
    sum_send,
    sum_recv,
    wide_send,
    wide_recv,
):
    col = lax.axis_index("frames")
    row = lax.axis_index("rows")
    per = frames // nf
    rows = frames * 8
    hist_len = hist_hbm.shape[0]
    tap_count = taps_ref.shape[1]

    load_start = pltpu.make_async_copy(start_hbm, start_f, local_sems.at[0])
    load_start.start()
    load_hist = pltpu.make_async_copy(hist_hbm, hist_v.at[pl.ds(0, hist_len)], local_sems.at[1])
    load_hist.start()
    load_taps = pltpu.make_async_copy(taps_hbm, taps_ref, local_sems.at[2])
    load_taps.start()
    load_half = pltpu.make_async_copy(half_hbm, half_ref, local_sems.at[3])
    load_half.start()

    barrier = pltpu.get_barrier_semaphore()

    def signal_frames(k, carry):
        pl.semaphore_signal(
            barrier, inc=1, device_id={"frames": lax.rem(col + k, nf)}, device_id_type=MESH
        )
        return carry

    def signal_rows(k, carry):
        pl.semaphore_signal(
            barrier, inc=1, device_id={"rows": lax.rem(row + k, nr)}, device_id_type=MESH
        )
        return carry

    lax.fori_loop(1, nf, signal_frames, 0)
    lax.fori_loop(1, nr, signal_rows, 0)
    exists = {}
    for dc in (-1, 0, 1):
        for dr in (-1, 0, 1):
            conds = []
            if dc == -1:
                conds.append(col > 0)
            if dc == 1:
                conds.append(col < nf - 1)
            if dr == -1:
                conds.append(row > 0)
            if dr == 1:
                conds.append(row < nr - 1)
            if conds:
                exists[dc, dr] = functools.reduce(jnp.logical_and, conds)
    for dc in (-1, 1):
        for dr in (-1, 1):

            @pl.when(exists[dc, dr])
            def _():
                pl.semaphore_signal(
                    barrier,
                    inc=1,
                    device_id={"frames": col + dc, "rows": row + dr},
                    device_id_type=MESH,
                )

    load_start.wait()
    for c in range(nf):
        high, low = split(start_f[:, :, :, c * 128 : (c + 1) * 128])
        hi_f[c] = high
        lo_f[c] = low

    sides = (col > 0).astype(jnp.int32) + (col < nf - 1).astype(jnp.int32)
    ends = (row > 0).astype(jnp.int32) + (row < nr - 1).astype(jnp.int32)
    pl.semaphore_wait(barrier, (nf - 1) + (nr - 1) + sides * ends)

    def order(k):
        return nf // 2 + ((k + 1) // 2) * (1 - 2 * lax.rem(k, 2))

    def exchange(index, source, target, own_source, own_target):
        own = pltpu.make_async_copy(own_source, own_target, a2a_recv.at[index])
        own.start()

        def send(k, carry):
            peer = lax.rem(col + order(k), nf)
            pltpu.make_async_remote_copy(
                src_ref=source(peer),
                dst_ref=target,
                send_sem=a2a_send.at[index],
                recv_sem=a2a_recv.at[index],
                device_id={"frames": peer},
                device_id_type=MESH,
            ).start()
            return carry

        lax.fori_loop(0, nf - 1, send, 0)

    def wait_bytes(view, sem):
        pltpu.make_async_copy(view, view, sem).wait()

    def to_block(index, source, buffer):
        target = buffer.at[pl.ds(col * per, per)]
        exchange(index, source, target, source(col), target)

    to_block(0, lambda c: hi_f.at[c], hi_c)
    to_block(1, lambda c: obs_hbm.at[:, :, :, pl.ds(pl.multiple_of(c * 128, 128), 128)], obs_c)

    def back_out(it):
        target = back_f.at[it, col]
        exchange(
            3 + it,
            lambda f: back_c.at[it, pl.ds(f * per, per)],
            target,
            back_c.at[it, pl.ds(col * per, per)],
            target,
        )

    def wide_copies(it, buffer):
        copies = [((0, -1), 0, below_f), ((0, 1), 1, above_f)]
        return [
            (
                where,
                pltpu.make_async_remote_copy(
                    src_ref=buffer.at[:, :, h],
                    dst_ref=target.at[it],
                    send_sem=wide_send.at[it, h],
                    recv_sem=wide_recv.at[it, h],
                    device_id={"rows": row + where[1]},
                    device_id_type=MESH,
                ),
            )
            for where, h, target in copies
        ]

    def start_all(copies):
        for where, copy in copies:

            @pl.when(exists[where])
            def _():
                copy.start()

    def recv_all(copies):
        for where, copy in copies:

            @pl.when(exists[-where[0], -where[1]])
            def _():
                copy.wait_recv()

    def send_all(copies):
        for where, copy in copies:

            @pl.when(exists[where])
            def _():
                copy.wait_send()

    start_all(wide_copies(0, hi_f))

    def clear(ref):
        ref[...] = jnp.zeros(ref.shape, BF16)

    @pl.when(row == 0)
    def _():
        clear(above)
        clear(above_f)
        clear(strips.at[:, 0])

    @pl.when(row == nr - 1)
    def _():
        clear(below)
        clear(below_f)
        clear(strips.at[:, 2])

    @pl.when(col == 0)
    def _():
        clear(strips.at[:, :, :, pl.ds(0, 128)])

    @pl.when(col == nf - 1)
    def _():
        clear(strips.at[:, :, :, pl.ds(128, 128)])

    hist_v[hist_len:] = jnp.zeros((hist_v.shape[0] - hist_len,) + hist_v.shape[1:], BF16)

    size = 256
    load_taps.wait()
    load_half.wait()
    spread = jnp.concatenate(
        [taps_ref[...].astype(F32), jnp.zeros((1, size - tap_count), F32)], axis=1
    )
    spread = jnp.broadcast_to(spread, (size, size))
    shifted = pltpu.roll(spread, size - (tap_count - 1), 1, stride=1, stride_axis=0).astype(BF16)
    at_t = onehot(iota((rows, size), 0) // 8 == iota((rows, size), 1))
    by_s = lax.dot_general(
        at_t, shifted, (((1,), (1,)), ((), ())), preferred_element_type=F32
    ).astype(BF16)

    def same_row(shape):
        return lax.rem(iota(shape, 0), 8) == lax.rem(iota(shape, 1), 8)

    hist_cols = kh.shape[1]
    s_of = iota((size, hist_cols), 0)
    pick = onehot((s_of == iota((size, hist_cols), 1) // 8) & (s_of < hist_len))
    kh[...] = jnp.where(same_row((rows, hist_cols)), dot(by_s, pick), 0.0).astype(BF16)
    pick = onehot(iota((size, rows), 0) == iota((size, rows), 1) // 8 + hist_len)
    kw[...] = jnp.where(same_row((rows, rows)), dot(by_s, pick), 0.0).astype(BF16)
    at_s = onehot(iota((rows, size), 0) // 8 + hist_len == iota((rows, size), 1))
    by_t = dot(at_s, shifted).astype(BF16)
    pick = onehot(iota((size, rows), 0) == iota((size, rows), 1) // 8)
    kwt[...] = jnp.where(same_row((rows, rows)), dot(by_t, pick), 0.0).astype(BF16)

    half = [half_ref[k] for k in range(half_ref.shape[0])]
    reach = half_ref.shape[0] - 1
    total = half[0]
    for k in range(1, reach + 1):
        total = total + 2.0 * half[k]
    total = jnp.full((1, 1), total, F32)
    scale = 1.0 / (total * total)

    def taps_at(distance):
        value = jnp.zeros(distance.shape, F32)
        for k in range(reach + 1):
            value = jnp.where(distance == k, half[k], value)
        return value

    high, low = split(taps_at(jnp.abs(iota((384, 128), 0) - 128 - iota((384, 128), 1))))
    band[:, 0:128] = high
    band[:, 128:256] = low

    rg = ah.shape[0]
    i0, i1 = iota((rg, rg), 0), iota((rg, rg), 1)
    for d in (-1, 0, 1):
        near = taps_at(jnp.abs(8 * d + lax.rem(i1, 8) - lax.rem(i0, 8)))
        high, low = split(jnp.where(i0 // 8 == i1 // 8, near, 0.0))
        ah[:, (d + 1) * rg : (d + 2) * rg] = high
        al[:, (d + 1) * rg : (d + 2) * rg] = low

    k0, k1 = iota((256, 256), 0), iota((256, 256), 1)
    place = lax.rem(k0, 128)
    inner, line = lax.rem(place, 8), lax.rem(k1, 128)
    near = taps_at(jnp.where(k0 < 128, line + 8 - inner, 128 + inner - line))
    near = jnp.where(lax.rem(place // 8, 2) == k1 // 128, near, 0.0)
    for g in range(GROUPS):
        high, low = split(jnp.where(place // 16 == g, near, 0.0))
        hbh[:, g * 256 : (g + 1) * 256] = high
        hbl[:, g * 256 : (g + 1) * 256] = low
    place = lax.rem(k1, 128)
    inner, line = lax.rem(place, 8), lax.rem(k0, 128)
    chosen = (lax.rem(place // 8, 2) == k0 // 128) & (line == jnp.where(k1 < 128, 120 + inner, inner))
    for g in range(GROUPS):
        sel[g * 256 : (g + 1) * 256, :] = onehot(chosen & (place // 16 == g))

    def halves(ref):
        parts = [ref[:, h].astype(F32).reshape(rows, 128) for h in (0, 1)]
        return jnp.concatenate(parts, axis=1)

    load_hist.wait()
    past = [hist_v[:, h].astype(F32).reshape(hist_cols, 128) for h in (0, 1)]
    past = dot(kh[...], jnp.concatenate(past, axis=1).astype(BF16))

    chunk = rows // GROUPS

    def edge_rows(n):
        cut = rows // 2 if n in CURVATURE else rows
        return pl.ds(0, cut), pl.ds(rows - cut, cut)

    def edge_copy(n, dr, part, slot):
        source, target = (edge_s.at[n, 0], below) if dr == -1 else (edge_s.at[n, 1], above)
        return (
            (0, dr),
            pltpu.make_async_remote_copy(
                src_ref=source.at[part],
                dst_ref=target.at[n, part],
                send_sem=halo_send.at[n, slot],
                recv_sem=halo_recv.at[n, slot],
                device_id={"rows": row + dr},
                device_id_type=MESH,
            ),
        )

    def rest_copies(n):
        half_rows = rows // 2
        return [
            edge_copy(n, -1, pl.ds(0, half_rows), 8),
            edge_copy(n, 1, pl.ds(half_rows, half_rows), 9),
        ]

    def halo_copies(n):
        upper, lower = edge_rows(n)
        result = [edge_copy(n, -1, lower, 1), edge_copy(n, 1, upper, 0)]
        copies = []
        for dc in (-1, 1):
            side = 0 if dc == 1 else 1
            for dr in (-1, 0, 1):
                copies.append(
                    (
                        (dc, dr),
                        strip_s.at[n, side],
                        strips.at[n, 1 - dr, :, pl.ds(side * 128, 128)],
                        2 + side * 3 + 1 - dr,
                    )
                )
        return result + [
            (
                where,
                pltpu.make_async_remote_copy(
                    src_ref=source,
                    dst_ref=target,
                    send_sem=halo_send.at[n, slot],
                    recv_sem=halo_recv.at[n, slot],
                    device_id={"frames": col + where[0], "rows": row + where[1]},
                    device_id_type=MESH,
                ),
            )
            for where, source, target, slot in copies
        ]

    def halo_start(n, field):
        edge_s[n, 0] = field[:, 0:128]
        edge_s[n, 1] = field[:, 128:256]
        wide = [field[g * chunk : (g + 1) * chunk, :] for g in range(GROUPS)]
        packed = dot(jnp.concatenate(wide, axis=1), sel[...]).astype(BF16)
        strip_s[n, 0] = packed[:, 0:128]
        strip_s[n, 1] = packed[:, 128:256]
        start_all(halo_copies(n))

    def smooth(n, field):
        if n in CURVATURE:
            cut = rows // 2
            gone, twice = jnp.zeros((cut, 128), BF16), jnp.asarray(2.0, BF16)
            outer = [above[n, 0:cut] * twice, gone], [gone, below[n, cut:rows] * twice]
        else:
            outer = [above[n]], [below[n]]
        stacked = jnp.concatenate(
            [*outer[0], field[:, 0:128], field[:, 128:256], *outer[1]], axis=0
        )
        wide = dot(stacked, band[128:256])
        flat = wide[:, 0:128] + wide[:, 128:256]
        lines = strips[n].reshape(3 * chunk, 256)
        corner = dot(lines, hbh[...]) + dot(lines, hbl[...])

        def part(block, which, h):
            extra = [
                corner[which * chunk : (which + 1) * chunk, g * 256 + h * 128 : g * 256 + h * 128 + 128]
                for g in range(GROUPS)
            ]
            if n in CURVATURE and which != 1:
                gone = jnp.zeros((chunk, 128), F32)
                kept = (0, 1, 2, 3) if which == 0 else (4, 5, 6, 7)
                extra = [2.0 * extra[g] if g in kept else gone for g in range(GROUPS)]
            return flat[block * rows : (block + 1) * rows] + jnp.concatenate(extra, axis=0)

        return along_rows([part(0, 0, 1), part(1, 1, 0), part(2, 1, 1), part(3, 2, 0)], n in CURVATURE)

    def smooth_wide(it, buffer):
        blocks = [above_f[it], buffer[:, :, 0], buffer[:, :, 1], below_f[it]]
        blocks = [b.astype(F32).reshape(rows, 128).astype(BF16) for b in blocks]
        step = 8 * per
        gap = jnp.zeros((step, 128), BF16)
        stacked = jnp.concatenate(
            [
                jnp.concatenate(
                    [
                        jnp.concatenate([gap, b[: rows - step]], axis=0),
                        b,
                        jnp.concatenate([b[step:], gap], axis=0),
                    ],
                    axis=1,
                )
                for b in blocks
            ],
            axis=0,
        )
        wide = dot(stacked, band[...])
        flat = wide[:, 0:128] + wide[:, 128:256]
        field = jnp.concatenate(blocks[1:3], axis=1).astype(F32)
        blocks = [flat[b * rows : (b + 1) * rows] for b in range(4)]
        pull_f[it] = REG_WEIGHT * (field - along_rows(blocks))

    def along_rows(blocks, coarse=False):
        pairs = [split(b) for b in blocks]
        result = []
        for q in range(rows // rg):
            cut = slice(q * rg, (q + 1) * rg)

            def tower(which):
                return jnp.concatenate(
                    [
                        jnp.concatenate([pairs[d][which][cut], pairs[d + 1][which][cut]], axis=1)
                        for d in range(3)
                    ],
                    axis=0,
                )

            high = tower(0)
            value = dot(ah[...], high) + dot(al[...], high)
            result.append(value if coarse else value + dot(ah[...], tower(1)))
        return jnp.concatenate(result, axis=0) * scale

    lane = iota((1, 128), 1)

    def sum_start(it, stage, value):
        axis, me, count = (("rows", row, nr), ("frames", col, nf))[stage]
        row_s[it, stage] = value
        row_r[it, stage, pl.ds(me, 1)] = value.reshape(1, 1, 128)

        def send(k, carry):
            pltpu.make_async_remote_copy(
                src_ref=row_s.at[it, stage],
                dst_ref=row_r.at[it, stage, me],
                send_sem=sum_send.at[it, stage],
                recv_sem=sum_recv.at[it, stage],
                device_id={axis: lax.rem(me + k, count)},
                device_id_type=MESH,
            ).start()
            return carry

        lax.fori_loop(1, count, send, 0)

    def sum_end(it, stage):
        count = (nr, nf)[stage]
        wait_bytes(row_r.at[it, stage, pl.ds(0, count - 1)], sum_recv.at[it, stage])
        return jnp.sum(row_r[it, stage], axis=0)

    def total_of(value):
        return jnp.sum(value, keepdims=True)

    recv_all(wide_copies(0, hi_f))
    smooth_wide(0, hi_f)

    def descend(point, pull, back, step):
        return jnp.maximum(point - step * (back + pull) - step * SPARSE_WEIGHT, 0.0)

    def wide_parts(c, h):
        cut = slice(c * 8 * per, (c + 1) * 8 * per)
        return cut, slice(h * 128, (h + 1) * 128)

    def update_first(step):
        wait_bytes(back_f.at[0], a2a_recv.at[3])
        for c in range(nf):
            for h in (0, 1):
                cut, lanes = wide_parts(c, h)
                where = slice(c * 128, (c + 1) * 128)
                point = start_f[:, h, :, where].reshape(8 * per, 128)
                back = back_f[0, c, :, h].astype(F32).reshape(8 * per, 128)
                updated = descend(point, pull_f[0, cut, lanes], back, step).reshape(per, 8, 128)
                first_f[:, h, :, where] = updated
                point_1[c, :, h] = updated.astype(BF16)
        start_all(wide_copies(1, point_1))
        store = pltpu.make_async_copy(first_f, out_first, store_sems.at[0])
        store.start()
        return store

    def slope_last():
        wait_bytes(back_f.at[1], a2a_recv.at[4])
        for c in range(nf):
            for h in (0, 1):
                cut, lanes = wide_parts(c, h)
                back = back_f[1, c, :, h].astype(F32).reshape(8 * per, 128)
                slope = (back + pull_f[1, cut, lanes]).reshape(per, 8, 128)
                slope_f[:, h, :, c * 128 : (c + 1) * 128] = slope
        store = pltpu.make_async_copy(slope_f, out_slope, store_sems.at[1])
        store.start()
        return store

    steps = []
    wait_bytes(hi_c, a2a_recv.at[0])
    point_bf = halves(hi_c).astype(BF16)
    halo_start(0, point_bf)
    to_block(2, lambda c: lo_f.at[c], lo_c)
    for it in range(ITERS):
        now = dot(kw[...], point_bf)
        if it == 0:
            wait_bytes(obs_c, a2a_recv.at[1])
            past = past - halves(obs_c)
        resid_bf = (past + now).astype(BF16)
        back = dot(kwt[...], resid_bf)
        for h in (0, 1):
            part = back[:, h * 128 : (h + 1) * 128].reshape(frames, 8, 128)
            back_c[it, :, h] = part.astype(BF16)
        back = back.astype(BF16).astype(F32)
        if it == 0:
            recv_all(halo_copies(0))
        point_f = point_bf.astype(F32)
        gradient = back + REG_WEIGHT * (point_f - smooth(2 * it, point_bf))
        grad_bf = gradient.astype(BF16)
        halo_start(2 * it + 1, grad_bf)
        back_out(it)
        if it == 0:
            start_all(rest_copies(1))
            halo_start(4, (gradient - grad_bf.astype(F32)).astype(BF16))
        conv = dot(kw[...], grad_bf)
        norm, conv = total_of(gradient * gradient), total_of(conv * conv)
        if it == 1:
            store_first = update_first(steps[0])
        recv_all(halo_copies(2 * it + 1))
        grad_smooth = smooth(2 * it + 1, grad_bf)
        grad_f32 = grad_bf.astype(F32)
        curv = total_of(grad_f32 * (grad_f32 - grad_smooth))
        sum_start(it, 0, jnp.where(lane == 0, norm, jnp.where(lane == 1, conv, curv)))
        if it == 0:
            wait_bytes(lo_c, a2a_recv.at[2])
            low = halves(lo_c)
            halo_start(5, low.astype(BF16))
        else:
            recv_all(wide_copies(1, point_1))
            smooth_wide(1, point_1)
        value = sum_end(it, 0)
        sum_start(it, 1, value)
        if it == 0:
            recv_all(rest_copies(1))
            recv_all(halo_copies(4))
            recv_all(halo_copies(5))
        else:
            store_slope = slope_last()
        value = sum_end(it, 1)
        step = value[:, 0:1] / (value[:, 1:2] + REG_WEIGHT * value[:, 2:3])
        steps.append(step)
        if it == 0:
            point = descend(halves(hi_c) + low, 0.0, gradient, step)
            point_bf = point.astype(BF16)
            for ref in (above, below, strips):
                start, slope = (
                    ref[high].astype(F32) + ref[low_part].astype(F32)
                    for high, low_part in ((0, 5), (1, 4))
                )
                ref[2] = descend(start, 0.0, slope, step).astype(BF16)
    out_step[...] = jnp.broadcast_to(step, out_step.shape)
    store_first.wait()
    store_slope.wait()

    wait_bytes(hi_f.at[pl.ds(0, nf - 1)], a2a_send.at[0])
    wait_bytes(obs_c.at[pl.ds(0, per * (nf - 1))], a2a_send.at[1])
    wait_bytes(lo_f.at[pl.ds(0, nf - 1)], a2a_send.at[2])
    for it in range(ITERS):
        wait_bytes(back_f.at[it, pl.ds(0, nf - 1)], a2a_send.at[3 + it])
        for stage, count in ((0, nr), (1, nf)):
            wait_bytes(row_r.at[it, stage, pl.ds(0, count - 1)], sum_send.at[it, stage])
        send_all(wide_copies(it, hi_f if it == 0 else point_1))
        for n in ((0, 1, 3), (4, 5))[it]:
            send_all(halo_copies(n))
    send_all(rest_copies(1))


def shards(nf, nr, observed, history, spikes_start, kernel, smooth_half):
    per, _, tall, cols = observed.shape
    frames = per * nf
    rows = frames * 8
    hist = history.shape[0]
    assert tall == 16 and history.shape[3] == 128 and cols == 128 * nf
    hist_pad = hist + 1
    rg = min(rows, 256)
    chunk = rows // GROUPS
    most = max(nf, nr)
    block = (per, 2, 8, 128)
    any_spec = pl.BlockSpec(memory_space=pltpu.MemorySpace.HBM)
    vmem = pl.BlockSpec(memory_space=pltpu.VMEM)
    out = jax.ShapeDtypeStruct((per, 2, 8, cols), F32)
    held = functools.partial(pltpu.with_memory_space_constraint, memory_space=pltpu.MemorySpace.HBM)
    first, slope, step = pl.pallas_call(
        functools.partial(body, nf, nr, frames),
        out_shape=(out, out, jax.ShapeDtypeStruct((1, 128), F32)),
        in_specs=[any_spec] * 5,
        out_specs=(any_spec, any_spec, vmem),
        scratch_shapes=[
            pltpu.VMEM((per, 2, 8, cols), F32),
            pltpu.VMEM((nf,) + block, BF16),
            pltpu.VMEM((nf,) + block, BF16),
            pltpu.VMEM((frames, 2, 8, 128), BF16),
            pltpu.VMEM((frames, 2, 8, 128), BF16),
            pltpu.VMEM((frames, 2, 8, 128), BF16),
            pltpu.VMEM((hist_pad, 2, 8, 128), BF16),
            pltpu.VMEM((ITERS, frames, 2, 8, 128), BF16),
            pltpu.VMEM((ITERS, nf) + block, BF16),
            pltpu.VMEM((nf,) + block, BF16),
            pltpu.VMEM((ITERS, nf, per, 8, 128), BF16),
            pltpu.VMEM((ITERS, nf, per, 8, 128), BF16),
            pltpu.VMEM((ITERS, rows, 256), F32),
            pltpu.VMEM((per, 2, 8, cols), F32),
            pltpu.VMEM((per, 2, 8, cols), F32),
            pltpu.SemaphoreType.DMA((2,)),
            pltpu.VMEM((1, kernel.shape[0]), BF16),
            pltpu.SMEM(smooth_half.shape, F32),
            pltpu.VMEM((HALOS, 2, rows, 128), BF16),
            pltpu.VMEM((HALOS, 2, chunk, 128), BF16),
            pltpu.VMEM((HALOS, rows, 128), BF16),
            pltpu.VMEM((HALOS, rows, 128), BF16),
            pltpu.VMEM((HALOS, 3, chunk, 256), BF16),
            pltpu.VMEM((ITERS, 2, 1, 128), F32),
            pltpu.VMEM((ITERS, 2, most, 1, 128), F32),
            pltpu.VMEM((rows, 8 * hist_pad), BF16),
            pltpu.VMEM((rows, rows), BF16),
            pltpu.VMEM((rows, rows), BF16),
            pltpu.VMEM((384, 256), BF16),
            pltpu.VMEM((rg, 3 * rg), BF16),
            pltpu.VMEM((rg, 3 * rg), BF16),
            pltpu.VMEM((GROUPS * 256, 256), BF16),
            pltpu.VMEM((256, GROUPS * 256), BF16),
            pltpu.VMEM((256, GROUPS * 256), BF16),
            pltpu.SemaphoreType.DMA((4,)),
            pltpu.SemaphoreType.DMA((3 + ITERS,)),
            pltpu.SemaphoreType.DMA((3 + ITERS,)),
            pltpu.SemaphoreType.DMA((HALOS, 10)),
            pltpu.SemaphoreType.DMA((HALOS, 10)),
            pltpu.SemaphoreType.DMA((ITERS, 2)),
            pltpu.SemaphoreType.DMA((ITERS, 2)),
            pltpu.SemaphoreType.DMA((ITERS, 2)),
            pltpu.SemaphoreType.DMA((ITERS, 2)),
        ],
        compiler_params=pltpu.CompilerParams(
            collective_id=0, has_side_effects=True, vmem_limit_bytes=44 * 1024 * 1024
        ),
        name="fista",
    )(
        held(observed.reshape(per, 2, 8, cols)),
        held(history.reshape(hist, 2, 8, 128)),
        held(spikes_start.reshape(per, 2, 8, cols)),
        held(kernel.reshape(1, -1)),
        held(smooth_half),
    )
    shape = spikes_start.shape
    step = step[0, 0]
    beta = momentum_terms(ITERS)[-1]
    first, slope = first.reshape(shape), slope.reshape(shape)
    spikes = jnp.maximum(first - step * slope - step * SPARSE_WEIGHT, 0.0)
    return spikes, spikes + beta * (spikes - first)


def solution(mesh):
    in_specs = (
        P("frames", None, "rows", None),
        P(None, None, "rows", "frames"),
        P("frames", None, "rows", None),
        P(),
        P(),
    )
    out_specs = (P("frames", None, "rows", None), P("frames", None, "rows", None))
    step = functools.partial(shards, mesh.shape["frames"], mesh.shape["rows"])
    return jax.shard_map(step, mesh=mesh, in_specs=in_specs, out_specs=out_specs, check_vma=False)
```

```python
import functools
import math

import jax
import jax.numpy as jnp
from jax import lax
from jax.experimental import pallas as pl
from jax.experimental.pallas import tpu as pltpu
from jax.sharding import PartitionSpec as P

ITERS = 2
REG_WEIGHT = 4.0
SPARSE_WEIGHT = 0.1
MESH = pl.DeviceIdType.MESH
F32 = jnp.float32
BF16 = jnp.bfloat16
GROUPS = 8
HALOS = 6
CURVATURE = (1, 3)


def momentum_terms(count):
    current = 1.0
    terms = []
    for iteration in range(count):
        upcoming = (1.0 + math.sqrt(1.0 + 4.0 * current * current)) / 2.0
        terms.append((current - 1.0) / upcoming)
        current = upcoming
    return terms


def iota(shape, dim):
    return lax.broadcasted_iota(jnp.int32, shape, dim)


def dot(a, b):
    return jnp.dot(a, b, preferred_element_type=F32)


def onehot(cond):
    return jnp.where(cond, 1.0, 0.0).astype(BF16)


def split(value):
    high = value.astype(BF16)
    return high, (value - high.astype(F32)).astype(BF16)


def body(
    nf,
    nr,
    frames,
    obs_hbm,
    hist_hbm,
    start_hbm,
    taps_hbm,
    half_hbm,
    out_first,
    out_slope,
    out_step,
    start_f,
    hi_f,
    lo_f,
    hi_c,
    lo_c,
    obs_c,
    hist_v,
    back_c,
    back_f,
    point_1,
    above_f,
    below_f,
    pull_f,
    first_f,
    slope_f,
    store_sems,
    taps_ref,
    half_ref,
    edge_s,
    strip_s,
    above,
    below,
    strips,
    row_s,
    row_r,
    kh,
    kw,
    kwt,
    band,
    ah,
    al,
    sel,
    hbh,
    hbl,
    local_sems,
    a2a_send,
    a2a_recv,
    halo_send,
    halo_recv,
    sum_send,
    sum_recv,
    wide_send,
    wide_recv,
):
    col = lax.axis_index("frames")
    row = lax.axis_index("rows")
    per = frames // nf
    rows = frames * 8
    hist_len = hist_hbm.shape[0]
    tap_count = taps_ref.shape[1]

    load_start = pltpu.make_async_copy(start_hbm, start_f, local_sems.at[0])
    load_start.start()
    load_hist = pltpu.make_async_copy(hist_hbm, hist_v.at[pl.ds(0, hist_len)], local_sems.at[1])
    load_hist.start()
    load_taps = pltpu.make_async_copy(taps_hbm, taps_ref, local_sems.at[2])
    load_taps.start()
    load_half = pltpu.make_async_copy(half_hbm, half_ref, local_sems.at[3])
    load_half.start()

    barrier = pltpu.get_barrier_semaphore()

    def signal_frames(k, carry):
        pl.semaphore_signal(
            barrier, inc=1, device_id={"frames": lax.rem(col + k, nf)}, device_id_type=MESH
        )
        return carry

    def signal_rows(k, carry):
        pl.semaphore_signal(
            barrier, inc=1, device_id={"rows": lax.rem(row + k, nr)}, device_id_type=MESH
        )
        return carry

    lax.fori_loop(1, nf, signal_frames, 0)
    lax.fori_loop(1, nr, signal_rows, 0)
    exists = {}
    for dc in (-1, 0, 1):
        for dr in (-1, 0, 1):
            conds = []
            if dc == -1:
                conds.append(col > 0)
            if dc == 1:
                conds.append(col < nf - 1)
            if dr == -1:
                conds.append(row > 0)
            if dr == 1:
                conds.append(row < nr - 1)
            if conds:
                exists[dc, dr] = functools.reduce(jnp.logical_and, conds)
    for dc in (-1, 1):
        for dr in (-1, 1):

            @pl.when(exists[dc, dr])
            def _():
                pl.semaphore_signal(
                    barrier,
                    inc=1,
                    device_id={"frames": col + dc, "rows": row + dr},
                    device_id_type=MESH,
                )

    load_start.wait()
    for c in range(nf):
        high, low = split(start_f[:, :, :, c * 128 : (c + 1) * 128])
        hi_f[c] = high
        lo_f[c] = low

    sides = (col > 0).astype(jnp.int32) + (col < nf - 1).astype(jnp.int32)
    ends = (row > 0).astype(jnp.int32) + (row < nr - 1).astype(jnp.int32)
    pl.semaphore_wait(barrier, (nf - 1) + (nr - 1) + sides * ends)

    def order(k):
        return nf // 2 + ((k + 1) // 2) * (1 - 2 * lax.rem(k, 2))

    def exchange(index, source, target, own_source, own_target):
        own = pltpu.make_async_copy(own_source, own_target, a2a_recv.at[index])
        own.start()

        def send(k, carry):
            peer = lax.rem(col + order(k), nf)
            pltpu.make_async_remote_copy(
                src_ref=source(peer),
                dst_ref=target,
                send_sem=a2a_send.at[index],
                recv_sem=a2a_recv.at[index],
                device_id={"frames": peer},
                device_id_type=MESH,
            ).start()
            return carry

        lax.fori_loop(0, nf - 1, send, 0)

    def wait_bytes(view, sem):
        pltpu.make_async_copy(view, view, sem).wait()

    def to_block(index, source, buffer):
        target = buffer.at[pl.ds(col * per, per)]
        exchange(index, source, target, source(col), target)

    to_block(0, lambda c: hi_f.at[c], hi_c)
    to_block(1, lambda c: obs_hbm.at[:, :, :, pl.ds(pl.multiple_of(c * 128, 128), 128)], obs_c)

    def back_out(it):
        target = back_f.at[it, col]
        exchange(
            3 + it,
            lambda f: back_c.at[it, pl.ds(f * per, per)],
            target,
            back_c.at[it, pl.ds(col * per, per)],
            target,
        )

    def wide_copies(it, buffer):
        copies = [((0, -1), 0, below_f), ((0, 1), 1, above_f)]
        return [
            (
                where,
                pltpu.make_async_remote_copy(
                    src_ref=buffer.at[:, :, h],
                    dst_ref=target.at[it],
                    send_sem=wide_send.at[it, h],
                    recv_sem=wide_recv.at[it, h],
                    device_id={"rows": row + where[1]},
                    device_id_type=MESH,
                ),
            )
            for where, h, target in copies
        ]

    def start_all(copies):
        for where, copy in copies:

            @pl.when(exists[where])
            def _():
                copy.start()

    def recv_all(copies):
        for where, copy in copies:

            @pl.when(exists[-where[0], -where[1]])
            def _():
                copy.wait_recv()

    def send_all(copies):
        for where, copy in copies:

            @pl.when(exists[where])
            def _():
                copy.wait_send()

    start_all(wide_copies(0, hi_f))

    def clear(ref):
        ref[...] = jnp.zeros(ref.shape, BF16)

    @pl.when(row == 0)
    def _():
        clear(above)
        clear(above_f)
        clear(strips.at[:, 0])

    @pl.when(row == nr - 1)
    def _():
        clear(below)
        clear(below_f)
        clear(strips.at[:, 2])

    @pl.when(col == 0)
    def _():
        clear(strips.at[:, :, :, pl.ds(0, 128)])

    @pl.when(col == nf - 1)
    def _():
        clear(strips.at[:, :, :, pl.ds(128, 128)])

    hist_v[hist_len:] = jnp.zeros((hist_v.shape[0] - hist_len,) + hist_v.shape[1:], BF16)

    size = 256
    load_taps.wait()
    load_half.wait()
    spread = jnp.concatenate(
        [taps_ref[...].astype(F32), jnp.zeros((1, size - tap_count), F32)], axis=1
    )
    spread = jnp.broadcast_to(spread, (size, size))
    shifted = pltpu.roll(spread, size - (tap_count - 1), 1, stride=1, stride_axis=0).astype(BF16)
    at_t = onehot(iota((rows, size), 0) // 8 == iota((rows, size), 1))
    by_s = lax.dot_general(
        at_t, shifted, (((1,), (1,)), ((), ())), preferred_element_type=F32
    ).astype(BF16)

    def same_row(shape):
        return lax.rem(iota(shape, 0), 8) == lax.rem(iota(shape, 1), 8)

    hist_cols = kh.shape[1]
    s_of = iota((size, hist_cols), 0)
    pick = onehot((s_of == iota((size, hist_cols), 1) // 8) & (s_of < hist_len))
    kh[...] = jnp.where(same_row((rows, hist_cols)), dot(by_s, pick), 0.0).astype(BF16)
    pick = onehot(iota((size, rows), 0) == iota((size, rows), 1) // 8 + hist_len)
    kw[...] = jnp.where(same_row((rows, rows)), dot(by_s, pick), 0.0).astype(BF16)
    at_s = onehot(iota((rows, size), 0) // 8 + hist_len == iota((rows, size), 1))
    by_t = dot(at_s, shifted).astype(BF16)
    pick = onehot(iota((size, rows), 0) == iota((size, rows), 1) // 8)
    kwt[...] = jnp.where(same_row((rows, rows)), dot(by_t, pick), 0.0).astype(BF16)

    half = [half_ref[k] for k in range(half_ref.shape[0])]
    reach = half_ref.shape[0] - 1
    total = half[0]
    for k in range(1, reach + 1):
        total = total + 2.0 * half[k]
    total = jnp.full((1, 1), total, F32)
    scale = 1.0 / (total * total)

    def taps_at(distance):
        value = jnp.zeros(distance.shape, F32)
        for k in range(reach + 1):
            value = jnp.where(distance == k, half[k], value)
        return value

    high, low = split(taps_at(jnp.abs(iota((384, 128), 0) - 128 - iota((384, 128), 1))))
    band[:, 0:128] = high
    band[:, 128:256] = low

    rg = ah.shape[0]
    i0, i1 = iota((rg, rg), 0), iota((rg, rg), 1)
    for d in (-1, 0, 1):
        near = taps_at(jnp.abs(8 * d + lax.rem(i1, 8) - lax.rem(i0, 8)))
        high, low = split(jnp.where(i0 // 8 == i1 // 8, near, 0.0))
        ah[:, (d + 1) * rg : (d + 2) * rg] = high
        al[:, (d + 1) * rg : (d + 2) * rg] = low

    k0, k1 = iota((256, 256), 0), iota((256, 256), 1)
    place = lax.rem(k0, 128)
    inner, line = lax.rem(place, 8), lax.rem(k1, 128)
    near = taps_at(jnp.where(k0 < 128, line + 8 - inner, 128 + inner - line))
    near = jnp.where(lax.rem(place // 8, 2) == k1 // 128, near, 0.0)
    for g in range(GROUPS):
        high, low = split(jnp.where(place // 16 == g, near, 0.0))
        hbh[:, g * 256 : (g + 1) * 256] = high
        hbl[:, g * 256 : (g + 1) * 256] = low
    place = lax.rem(k1, 128)
    inner, line = lax.rem(place, 8), lax.rem(k0, 128)
    chosen = (lax.rem(place // 8, 2) == k0 // 128) & (line == jnp.where(k1 < 128, 120 + inner, inner))
    for g in range(GROUPS):
        sel[g * 256 : (g + 1) * 256, :] = onehot(chosen & (place // 16 == g))

    def halves(ref):
        parts = [ref[:, h].astype(F32).reshape(rows, 128) for h in (0, 1)]
        return jnp.concatenate(parts, axis=1)

    load_hist.wait()
    past = [hist_v[:, h].astype(F32).reshape(hist_cols, 128) for h in (0, 1)]
    past = dot(kh[...], jnp.concatenate(past, axis=1).astype(BF16))

    chunk = rows // GROUPS

    def edge_rows(n):
        cut = rows // 2 if n in CURVATURE else rows
        return pl.ds(0, cut), pl.ds(rows - cut, cut)

    def edge_copy(n, dr, part, slot):
        source, target = (edge_s.at[n, 0], below) if dr == -1 else (edge_s.at[n, 1], above)
        return (
            (0, dr),
            pltpu.make_async_remote_copy(
                src_ref=source.at[part],
                dst_ref=target.at[n, part],
                send_sem=halo_send.at[n, slot],
                recv_sem=halo_recv.at[n, slot],
                device_id={"rows": row + dr},
                device_id_type=MESH,
            ),
        )

    def rest_copies(n):
        half_rows = rows // 2
        return [
            edge_copy(n, -1, pl.ds(0, half_rows), 8),
            edge_copy(n, 1, pl.ds(half_rows, half_rows), 9),
        ]

    def halo_copies(n):
        upper, lower = edge_rows(n)
        result = [edge_copy(n, -1, lower, 1), edge_copy(n, 1, upper, 0)]
        copies = []
        for dc in (-1, 1):
            side = 0 if dc == 1 else 1
            for dr in (-1, 0, 1):
                copies.append(
                    (
                        (dc, dr),
                        strip_s.at[n, side],
                        strips.at[n, 1 - dr, :, pl.ds(side * 128, 128)],
                        2 + side * 3 + 1 - dr,
                    )
                )
        return result + [
            (
                where,
                pltpu.make_async_remote_copy(
                    src_ref=source,
                    dst_ref=target,
                    send_sem=halo_send.at[n, slot],
                    recv_sem=halo_recv.at[n, slot],
                    device_id={"frames": col + where[0], "rows": row + where[1]},
                    device_id_type=MESH,
                ),
            )
            for where, source, target, slot in copies
        ]

    def halo_start(n, field):
        edge_s[n, 0] = field[:, 0:128]
        edge_s[n, 1] = field[:, 128:256]
        copies = halo_copies(n)
        start_all(copies[:2])
        wide = [field[g * chunk : (g + 1) * chunk, :] for g in range(GROUPS)]
        packed = dot(jnp.concatenate(wide, axis=1), sel[...]).astype(BF16)
        strip_s[n, 0] = packed[:, 0:128]
        strip_s[n, 1] = packed[:, 128:256]
        start_all(copies[2:])

    def smooth(n, field):
        if n in CURVATURE:
            cut = rows // 2
            gone, twice = jnp.zeros((cut, 128), BF16), jnp.asarray(2.0, BF16)
            outer = [above[n, 0:cut] * twice, gone], [gone, below[n, cut:rows] * twice]
        else:
            outer = [above[n]], [below[n]]
        stacked = jnp.concatenate(
            [*outer[0], field[:, 0:128], field[:, 128:256], *outer[1]], axis=0
        )
        wide = dot(stacked, band[128:256])
        flat = wide[:, 0:128] + wide[:, 128:256]
        lines = strips[n].reshape(3 * chunk, 256)
        corner = dot(lines, hbh[...]) + dot(lines, hbl[...])

        def part(block, which, h):
            extra = [
                corner[which * chunk : (which + 1) * chunk, g * 256 + h * 128 : g * 256 + h * 128 + 128]
                for g in range(GROUPS)
            ]
            if n in CURVATURE and which != 1:
                gone = jnp.zeros((chunk, 128), F32)
                kept = (0, 1, 2, 3) if which == 0 else (4, 5, 6, 7)
                extra = [2.0 * extra[g] if g in kept else gone for g in range(GROUPS)]
            return flat[block * rows : (block + 1) * rows] + jnp.concatenate(extra, axis=0)

        return along_rows([part(0, 0, 1), part(1, 1, 0), part(2, 1, 1), part(3, 2, 0)], n in CURVATURE)

    def smooth_wide(it, buffer):
        blocks = [above_f[it], buffer[:, :, 0], buffer[:, :, 1], below_f[it]]
        blocks = [b.astype(F32).reshape(rows, 128).astype(BF16) for b in blocks]
        step = 8 * per
        gap = jnp.zeros((step, 128), BF16)
        stacked = jnp.concatenate(
            [
                jnp.concatenate(
                    [
                        jnp.concatenate([gap, b[: rows - step]], axis=0),
                        b,
                        jnp.concatenate([b[step:], gap], axis=0),
                    ],
                    axis=1,
                )
                for b in blocks
            ],
            axis=0,
        )
        wide = dot(stacked, band[...])
        flat = wide[:, 0:128] + wide[:, 128:256]
        field = jnp.concatenate(blocks[1:3], axis=1).astype(F32)
        blocks = [flat[b * rows : (b + 1) * rows] for b in range(4)]
        pull_f[it] = REG_WEIGHT * (field - along_rows(blocks))

    def along_rows(blocks, coarse=False):
        pairs = [split(b) for b in blocks]
        result = []
        for q in range(rows // rg):
            cut = slice(q * rg, (q + 1) * rg)

            def tower(which):
                return jnp.concatenate(
                    [
                        jnp.concatenate([pairs[d][which][cut], pairs[d + 1][which][cut]], axis=1)
                        for d in range(3)
                    ],
                    axis=0,
                )

            high = tower(0)
            value = dot(ah[...], high) + dot(al[...], high)
            result.append(value if coarse else value + dot(ah[...], tower(1)))
        return jnp.concatenate(result, axis=0) * scale

    lane = iota((1, 128), 1)

    def sum_start(it, stage, value):
        axis, me, count = (("rows", row, nr), ("frames", col, nf))[stage]
        row_s[it, stage] = value
        row_r[it, stage, pl.ds(me, 1)] = value.reshape(1, 1, 128)

        def send(k, carry):
            pltpu.make_async_remote_copy(
                src_ref=row_s.at[it, stage],
                dst_ref=row_r.at[it, stage, me],
                send_sem=sum_send.at[it, stage],
                recv_sem=sum_recv.at[it, stage],
                device_id={axis: lax.rem(me + k, count)},
                device_id_type=MESH,
            ).start()
            return carry

        lax.fori_loop(1, count, send, 0)

    def sum_end(it, stage):
        count = (nr, nf)[stage]
        wait_bytes(row_r.at[it, stage, pl.ds(0, count - 1)], sum_recv.at[it, stage])
        return jnp.sum(row_r[it, stage], axis=0)

    def total_of(value):
        return jnp.sum(value, keepdims=True)

    recv_all(wide_copies(0, hi_f))
    smooth_wide(0, hi_f)

    def descend(point, pull, back, step):
        return jnp.maximum(point - step * (back + pull) - step * SPARSE_WEIGHT, 0.0)

    def wide_parts(c, h):
        cut = slice(c * 8 * per, (c + 1) * 8 * per)
        return cut, slice(h * 128, (h + 1) * 128)

    def update_first(step):
        wait_bytes(back_f.at[0], a2a_recv.at[3])
        for c in range(nf):
            for h in (0, 1):
                cut, lanes = wide_parts(c, h)
                where = slice(c * 128, (c + 1) * 128)
                point = start_f[:, h, :, where].reshape(8 * per, 128)
                back = back_f[0, c, :, h].astype(F32).reshape(8 * per, 128)
                updated = descend(point, pull_f[0, cut, lanes], back, step).reshape(per, 8, 128)
                first_f[:, h, :, where] = updated
                point_1[c, :, h] = updated.astype(BF16)
        start_all(wide_copies(1, point_1))
        store = pltpu.make_async_copy(first_f, out_first, store_sems.at[0])
        store.start()
        return store

    def slope_last():
        wait_bytes(back_f.at[1], a2a_recv.at[4])
        for c in range(nf):
            for h in (0, 1):
                cut, lanes = wide_parts(c, h)
                back = back_f[1, c, :, h].astype(F32).reshape(8 * per, 128)
                slope = (back + pull_f[1, cut, lanes]).reshape(per, 8, 128)
                slope_f[:, h, :, c * 128 : (c + 1) * 128] = slope
        store = pltpu.make_async_copy(slope_f, out_slope, store_sems.at[1])
        store.start()
        return store

    steps = []
    wait_bytes(hi_c, a2a_recv.at[0])
    point_bf = halves(hi_c).astype(BF16)
    halo_start(0, point_bf)
    to_block(2, lambda c: lo_f.at[c], lo_c)
    for it in range(ITERS):
        now = dot(kw[...], point_bf)
        if it == 0:
            wait_bytes(obs_c, a2a_recv.at[1])
            past = past - halves(obs_c)
        resid_bf = (past + now).astype(BF16)
        back = dot(kwt[...], resid_bf)
        for h in (0, 1):
            part = back[:, h * 128 : (h + 1) * 128].reshape(frames, 8, 128)
            back_c[it, :, h] = part.astype(BF16)
        back = back.astype(BF16).astype(F32)
        if it == 0:
            recv_all(halo_copies(0))
        point_f = point_bf.astype(F32)
        gradient = back + REG_WEIGHT * (point_f - smooth(2 * it, point_bf))
        grad_bf = gradient.astype(BF16)
        halo_start(2 * it + 1, grad_bf)
        back_out(it)
        if it == 0:
            start_all(rest_copies(1))
            halo_start(4, (gradient - grad_bf.astype(F32)).astype(BF16))
        conv = dot(kw[...], grad_bf)
        norm, conv = total_of(gradient * gradient), total_of(conv * conv)
        if it == 1:
            store_first = update_first(steps[0])
        recv_all(halo_copies(2 * it + 1))
        grad_smooth = smooth(2 * it + 1, grad_bf)
        grad_f32 = grad_bf.astype(F32)
        curv = total_of(grad_f32 * (grad_f32 - grad_smooth))
        sum_start(it, 0, jnp.where(lane == 0, norm, jnp.where(lane == 1, conv, curv)))
        if it == 0:
            wait_bytes(lo_c, a2a_recv.at[2])
            low = halves(lo_c)
            halo_start(5, low.astype(BF16))
        else:
            recv_all(wide_copies(1, point_1))
            smooth_wide(1, point_1)
        value = sum_end(it, 0)
        sum_start(it, 1, value)
        if it == 0:
            recv_all(rest_copies(1))
            recv_all(halo_copies(4))
            recv_all(halo_copies(5))
        else:
            store_slope = slope_last()
        value = sum_end(it, 1)
        step = value[:, 0:1] / (value[:, 1:2] + REG_WEIGHT * value[:, 2:3])
        steps.append(step)
        if it == 0:
            point = descend(halves(hi_c) + low, 0.0, gradient, step)
            point_bf = point.astype(BF16)
            for ref in (above, below, strips):
                start, slope = (
                    ref[high].astype(F32) + ref[low_part].astype(F32)
                    for high, low_part in ((0, 5), (1, 4))
                )
                ref[2] = descend(start, 0.0, slope, step).astype(BF16)
    out_step[...] = jnp.broadcast_to(step, out_step.shape)
    store_first.wait()
    store_slope.wait()

    wait_bytes(hi_f.at[pl.ds(0, nf - 1)], a2a_send.at[0])
    wait_bytes(obs_c.at[pl.ds(0, per * (nf - 1))], a2a_send.at[1])
    wait_bytes(lo_f.at[pl.ds(0, nf - 1)], a2a_send.at[2])
    for it in range(ITERS):
        wait_bytes(back_f.at[it, pl.ds(0, nf - 1)], a2a_send.at[3 + it])
        for stage, count in ((0, nr), (1, nf)):
            wait_bytes(row_r.at[it, stage, pl.ds(0, count - 1)], sum_send.at[it, stage])
        send_all(wide_copies(it, hi_f if it == 0 else point_1))
        for n in ((0, 1, 3), (4, 5))[it]:
            send_all(halo_copies(n))
    send_all(rest_copies(1))


def shards(nf, nr, observed, history, spikes_start, kernel, smooth_half):
    per, _, tall, cols = observed.shape
    frames = per * nf
    rows = frames * 8
    hist = history.shape[0]
    assert tall == 16 and history.shape[3] == 128 and cols == 128 * nf
    hist_pad = hist + 1
    rg = min(rows, 256)
    chunk = rows // GROUPS
    most = max(nf, nr)
    block = (per, 2, 8, 128)
    any_spec = pl.BlockSpec(memory_space=pltpu.MemorySpace.HBM)
    vmem = pl.BlockSpec(memory_space=pltpu.VMEM)
    out = jax.ShapeDtypeStruct((per, 2, 8, cols), F32)
    held = functools.partial(pltpu.with_memory_space_constraint, memory_space=pltpu.MemorySpace.HBM)
    first, slope, step = pl.pallas_call(
        functools.partial(body, nf, nr, frames),
        out_shape=(out, out, jax.ShapeDtypeStruct((1, 128), F32)),
        in_specs=[any_spec] * 5,
        out_specs=(any_spec, any_spec, vmem),
        scratch_shapes=[
            pltpu.VMEM((per, 2, 8, cols), F32),
            pltpu.VMEM((nf,) + block, BF16),
            pltpu.VMEM((nf,) + block, BF16),
            pltpu.VMEM((frames, 2, 8, 128), BF16),
            pltpu.VMEM((frames, 2, 8, 128), BF16),
            pltpu.VMEM((frames, 2, 8, 128), BF16),
            pltpu.VMEM((hist_pad, 2, 8, 128), BF16),
            pltpu.VMEM((ITERS, frames, 2, 8, 128), BF16),
            pltpu.VMEM((ITERS, nf) + block, BF16),
            pltpu.VMEM((nf,) + block, BF16),
            pltpu.VMEM((ITERS, nf, per, 8, 128), BF16),
            pltpu.VMEM((ITERS, nf, per, 8, 128), BF16),
            pltpu.VMEM((ITERS, rows, 256), F32),
            pltpu.VMEM((per, 2, 8, cols), F32),
            pltpu.VMEM((per, 2, 8, cols), F32),
            pltpu.SemaphoreType.DMA((2,)),
            pltpu.VMEM((1, kernel.shape[0]), BF16),
            pltpu.SMEM(smooth_half.shape, F32),
            pltpu.VMEM((HALOS, 2, rows, 128), BF16),
            pltpu.VMEM((HALOS, 2, chunk, 128), BF16),
            pltpu.VMEM((HALOS, rows, 128), BF16),
            pltpu.VMEM((HALOS, rows, 128), BF16),
            pltpu.VMEM((HALOS, 3, chunk, 256), BF16),
            pltpu.VMEM((ITERS, 2, 1, 128), F32),
            pltpu.VMEM((ITERS, 2, most, 1, 128), F32),
            pltpu.VMEM((rows, 8 * hist_pad), BF16),
            pltpu.VMEM((rows, rows), BF16),
            pltpu.VMEM((rows, rows), BF16),
            pltpu.VMEM((384, 256), BF16),
            pltpu.VMEM((rg, 3 * rg), BF16),
            pltpu.VMEM((rg, 3 * rg), BF16),
            pltpu.VMEM((GROUPS * 256, 256), BF16),
            pltpu.VMEM((256, GROUPS * 256), BF16),
            pltpu.VMEM((256, GROUPS * 256), BF16),
            pltpu.SemaphoreType.DMA((4,)),
            pltpu.SemaphoreType.DMA((3 + ITERS,)),
            pltpu.SemaphoreType.DMA((3 + ITERS,)),
            pltpu.SemaphoreType.DMA((HALOS, 10)),
            pltpu.SemaphoreType.DMA((HALOS, 10)),
            pltpu.SemaphoreType.DMA((ITERS, 2)),
            pltpu.SemaphoreType.DMA((ITERS, 2)),
            pltpu.SemaphoreType.DMA((ITERS, 2)),
            pltpu.SemaphoreType.DMA((ITERS, 2)),
        ],
        compiler_params=pltpu.CompilerParams(
            collective_id=0, has_side_effects=True, vmem_limit_bytes=44 * 1024 * 1024
        ),
        name="fista",
    )(
        held(observed.reshape(per, 2, 8, cols)),
        held(history.reshape(hist, 2, 8, 128)),
        held(spikes_start.reshape(per, 2, 8, cols)),
        held(kernel.reshape(1, -1)),
        held(smooth_half),
    )
    shape = spikes_start.shape
    step = step[0, 0]
    beta = momentum_terms(ITERS)[-1]
    first, slope = first.reshape(shape), slope.reshape(shape)
    spikes = jnp.maximum(first - step * slope - step * SPARSE_WEIGHT, 0.0)
    return spikes, spikes + beta * (spikes - first)


def solution(mesh):
    in_specs = (
        P("frames", None, "rows", None),
        P(None, None, "rows", "frames"),
        P("frames", None, "rows", None),
        P(),
        P(),
    )
    out_specs = (P("frames", None, "rows", None), P("frames", None, "rows", None))
    step = functools.partial(shards, mesh.shape["frames"], mesh.shape["rows"])
    return jax.shard_map(step, mesh=mesh, in_specs=in_specs, out_specs=out_specs, check_vma=False)
```

```python
import functools
import math

import jax
import jax.numpy as jnp
from jax import lax
from jax.experimental import pallas as pl
from jax.experimental.pallas import tpu as pltpu
from jax.sharding import PartitionSpec as P

ITERS = 2
REG_WEIGHT = 4.0
SPARSE_WEIGHT = 0.1
MESH = pl.DeviceIdType.MESH
F32 = jnp.float32
BF16 = jnp.bfloat16
GROUPS = 8
HALOS = 6
CURVATURE = (1, 3)


def momentum_terms(count):
    current = 1.0
    terms = []
    for iteration in range(count):
        upcoming = (1.0 + math.sqrt(1.0 + 4.0 * current * current)) / 2.0
        terms.append((current - 1.0) / upcoming)
        current = upcoming
    return terms


def iota(shape, dim):
    return lax.broadcasted_iota(jnp.int32, shape, dim)


def dot(a, b):
    return jnp.dot(a, b, preferred_element_type=F32)


def onehot(cond):
    return jnp.where(cond, 1.0, 0.0).astype(BF16)


def split(value):
    high = value.astype(BF16)
    return high, (value - high.astype(F32)).astype(BF16)


def body(
    nf,
    nr,
    frames,
    obs_hbm,
    hist_hbm,
    start_hbm,
    taps_hbm,
    half_hbm,
    out_first,
    out_slope,
    out_step,
    start_f,
    hi_f,
    lo_f,
    hi_c,
    lo_c,
    obs_c,
    hist_v,
    back_c,
    back_f,
    point_1,
    above_f,
    below_f,
    pull_f,
    first_f,
    slope_f,
    store_sems,
    taps_ref,
    half_ref,
    edge_s,
    strip_s,
    above,
    below,
    strips,
    row_s,
    row_r,
    kh,
    kw,
    kwt,
    band,
    ah,
    al,
    sel,
    hbh,
    hbl,
    local_sems,
    a2a_send,
    a2a_recv,
    halo_send,
    halo_recv,
    sum_send,
    sum_recv,
    wide_send,
    wide_recv,
):
    col = lax.axis_index("frames")
    row = lax.axis_index("rows")
    per = frames // nf
    rows = frames * 8
    hist_len = hist_hbm.shape[0]
    tap_count = taps_ref.shape[1]

    load_start = pltpu.make_async_copy(start_hbm, start_f, local_sems.at[0])
    load_start.start()
    load_hist = pltpu.make_async_copy(hist_hbm, hist_v.at[pl.ds(0, hist_len)], local_sems.at[1])
    load_hist.start()
    load_taps = pltpu.make_async_copy(taps_hbm, taps_ref, local_sems.at[2])
    load_taps.start()
    load_half = pltpu.make_async_copy(half_hbm, half_ref, local_sems.at[3])
    load_half.start()

    barrier = pltpu.get_barrier_semaphore()

    def signal_frames(k, carry):
        pl.semaphore_signal(
            barrier, inc=1, device_id={"frames": lax.rem(col + k, nf)}, device_id_type=MESH
        )
        return carry

    def signal_rows(k, carry):
        pl.semaphore_signal(
            barrier, inc=1, device_id={"rows": lax.rem(row + k, nr)}, device_id_type=MESH
        )
        return carry

    lax.fori_loop(1, nf, signal_frames, 0)
    lax.fori_loop(1, nr, signal_rows, 0)
    exists = {}
    for dc in (-1, 0, 1):
        for dr in (-1, 0, 1):
            conds = []
            if dc == -1:
                conds.append(col > 0)
            if dc == 1:
                conds.append(col < nf - 1)
            if dr == -1:
                conds.append(row > 0)
            if dr == 1:
                conds.append(row < nr - 1)
            if conds:
                exists[dc, dr] = functools.reduce(jnp.logical_and, conds)
    for dc in (-1, 1):
        for dr in (-1, 1):

            @pl.when(exists[dc, dr])
            def _():
                pl.semaphore_signal(
                    barrier,
                    inc=1,
                    device_id={"frames": col + dc, "rows": row + dr},
                    device_id_type=MESH,
                )

    load_start.wait()
    for c in range(nf):
        high, low = split(start_f[:, :, :, c * 128 : (c + 1) * 128])
        hi_f[c] = high
        lo_f[c] = low

    sides = (col > 0).astype(jnp.int32) + (col < nf - 1).astype(jnp.int32)
    ends = (row > 0).astype(jnp.int32) + (row < nr - 1).astype(jnp.int32)
    pl.semaphore_wait(barrier, (nf - 1) + (nr - 1) + sides * ends)

    def order(k):
        return nf // 2 + ((k + 1) // 2) * (1 - 2 * lax.rem(k, 2))

    def exchange(index, source, target, own_source, own_target):
        own = pltpu.make_async_copy(own_source, own_target, a2a_recv.at[index])
        own.start()

        def send(k, carry):
            peer = lax.rem(col + order(k), nf)
            pltpu.make_async_remote_copy(
                src_ref=source(peer),
                dst_ref=target,
                send_sem=a2a_send.at[index],
                recv_sem=a2a_recv.at[index],
                device_id={"frames": peer},
                device_id_type=MESH,
            ).start()
            return carry

        lax.fori_loop(0, nf - 1, send, 0)

    def wait_bytes(view, sem):
        pltpu.make_async_copy(view, view, sem).wait()

    def to_block(index, source, buffer):
        target = buffer.at[pl.ds(col * per, per)]
        exchange(index, source, target, source(col), target)

    to_block(0, lambda c: hi_f.at[c], hi_c)
    to_block(1, lambda c: obs_hbm.at[:, :, :, pl.ds(pl.multiple_of(c * 128, 128), 128)], obs_c)

    def back_out(it):
        target = back_f.at[it, col]
        exchange(
            3 + it,
            lambda f: back_c.at[it, pl.ds(f * per, per)],
            target,
            back_c.at[it, pl.ds(col * per, per)],
            target,
        )

    def wide_copies(it, buffer):
        copies = [((0, -1), 0, below_f), ((0, 1), 1, above_f)]
        return [
            (
                where,
                pltpu.make_async_remote_copy(
                    src_ref=buffer.at[:, :, h],
                    dst_ref=target.at[it],
                    send_sem=wide_send.at[it, h],
                    recv_sem=wide_recv.at[it, h],
                    device_id={"rows": row + where[1]},
                    device_id_type=MESH,
                ),
            )
            for where, h, target in copies
        ]

    def start_all(copies):
        for where, copy in copies:

            @pl.when(exists[where])
            def _():
                copy.start()

    def recv_all(copies):
        for where, copy in copies:

            @pl.when(exists[-where[0], -where[1]])
            def _():
                copy.wait_recv()

    def send_all(copies):
        for where, copy in copies:

            @pl.when(exists[where])
            def _():
                copy.wait_send()

    start_all(wide_copies(0, hi_f))

    def clear(ref):
        ref[...] = jnp.zeros(ref.shape, BF16)

    @pl.when(row == 0)
    def _():
        clear(above)
        clear(above_f)
        clear(strips.at[:, 0])

    @pl.when(row == nr - 1)
    def _():
        clear(below)
        clear(below_f)
        clear(strips.at[:, 2])

    @pl.when(col == 0)
    def _():
        clear(strips.at[:, :, :, pl.ds(0, 128)])

    @pl.when(col == nf - 1)
    def _():
        clear(strips.at[:, :, :, pl.ds(128, 128)])

    hist_v[hist_len:] = jnp.zeros((hist_v.shape[0] - hist_len,) + hist_v.shape[1:], BF16)

    size = 256
    load_taps.wait()
    load_half.wait()
    spread = jnp.concatenate(
        [taps_ref[...].astype(F32), jnp.zeros((1, size - tap_count), F32)], axis=1
    )
    spread = jnp.broadcast_to(spread, (size, size))
    shifted = pltpu.roll(spread, size - (tap_count - 1), 1, stride=1, stride_axis=0).astype(BF16)
    at_t = onehot(iota((rows, size), 0) // 8 == iota((rows, size), 1))
    by_s = lax.dot_general(
        at_t, shifted, (((1,), (1,)), ((), ())), preferred_element_type=F32
    ).astype(BF16)

    def same_row(shape):
        return lax.rem(iota(shape, 0), 8) == lax.rem(iota(shape, 1), 8)

    hist_cols = kh.shape[1]
    s_of = iota((size, hist_cols), 0)
    pick = onehot((s_of == iota((size, hist_cols), 1) // 8) & (s_of < hist_len))
    kh[...] = jnp.where(same_row((rows, hist_cols)), dot(by_s, pick), 0.0).astype(BF16)
    pick = onehot(iota((size, rows), 0) == iota((size, rows), 1) // 8 + hist_len)
    kw[...] = jnp.where(same_row((rows, rows)), dot(by_s, pick), 0.0).astype(BF16)
    at_s = onehot(iota((rows, size), 0) // 8 + hist_len == iota((rows, size), 1))
    by_t = dot(at_s, shifted).astype(BF16)
    pick = onehot(iota((size, rows), 0) == iota((size, rows), 1) // 8)
    kwt[...] = jnp.where(same_row((rows, rows)), dot(by_t, pick), 0.0).astype(BF16)

    half = [half_ref[k] for k in range(half_ref.shape[0])]
    reach = half_ref.shape[0] - 1
    total = half[0]
    for k in range(1, reach + 1):
        total = total + 2.0 * half[k]
    total = jnp.full((1, 1), total, F32)
    scale = 1.0 / (total * total)

    def taps_at(distance):
        value = jnp.zeros(distance.shape, F32)
        for k in range(reach + 1):
            value = jnp.where(distance == k, half[k], value)
        return value

    high, low = split(taps_at(jnp.abs(iota((384, 128), 0) - 128 - iota((384, 128), 1))))
    band[:, 0:128] = high
    band[:, 128:256] = low

    rg = ah.shape[0]
    i0, i1 = iota((rg, rg), 0), iota((rg, rg), 1)
    for d in (-1, 0, 1):
        near = taps_at(jnp.abs(8 * d + lax.rem(i1, 8) - lax.rem(i0, 8)))
        high, low = split(jnp.where(i0 // 8 == i1 // 8, near, 0.0))
        ah[:, (d + 1) * rg : (d + 2) * rg] = high
        al[:, (d + 1) * rg : (d + 2) * rg] = low

    k0, k1 = iota((256, 256), 0), iota((256, 256), 1)
    place = lax.rem(k0, 128)
    inner, line = lax.rem(place, 8), lax.rem(k1, 128)
    near = taps_at(jnp.where(k0 < 128, line + 8 - inner, 128 + inner - line))
    near = jnp.where(lax.rem(place // 8, 2) == k1 // 128, near, 0.0)
    for g in range(GROUPS):
        high, low = split(jnp.where(place // 16 == g, near, 0.0))
        hbh[:, g * 256 : (g + 1) * 256] = high
        hbl[:, g * 256 : (g + 1) * 256] = low
    place = lax.rem(k1, 128)
    inner, line = lax.rem(place, 8), lax.rem(k0, 128)
    chosen = (lax.rem(place // 8, 2) == k0 // 128) & (line == jnp.where(k1 < 128, 120 + inner, inner))
    for g in range(GROUPS):
        sel[g * 256 : (g + 1) * 256, :] = onehot(chosen & (place // 16 == g))

    def halves(ref):
        parts = [ref[:, h].astype(F32).reshape(rows, 128) for h in (0, 1)]
        return jnp.concatenate(parts, axis=1)

    load_hist.wait()
    past = [hist_v[:, h].astype(F32).reshape(hist_cols, 128) for h in (0, 1)]
    past = dot(kh[...], jnp.concatenate(past, axis=1).astype(BF16))

    chunk = rows // GROUPS

    def edge_rows(n):
        cut = rows // 2 if n in CURVATURE else rows
        return pl.ds(0, cut), pl.ds(rows - cut, cut)

    def edge_copy(n, dr, part, slot):
        source, target = (edge_s.at[n, 0], below) if dr == -1 else (edge_s.at[n, 1], above)
        return (
            (0, dr),
            pltpu.make_async_remote_copy(
                src_ref=source.at[part],
                dst_ref=target.at[n, part],
                send_sem=halo_send.at[n, slot],
                recv_sem=halo_recv.at[n, slot],
                device_id={"rows": row + dr},
                device_id_type=MESH,
            ),
        )

    def rest_copies(n):
        half_rows = rows // 2
        return [
            edge_copy(n, -1, pl.ds(0, half_rows), 8),
            edge_copy(n, 1, pl.ds(half_rows, half_rows), 9),
        ]

    def halo_copies(n):
        upper, lower = edge_rows(n)
        result = [edge_copy(n, -1, lower, 1), edge_copy(n, 1, upper, 0)]
        copies = []
        for dc in (-1, 1):
            side = 0 if dc == 1 else 1
            for dr in (-1, 0, 1):
                copies.append(
                    (
                        (dc, dr),
                        strip_s.at[n, side],
                        strips.at[n, 1 - dr, :, pl.ds(side * 128, 128)],
                        2 + side * 3 + 1 - dr,
                    )
                )
        return result + [
            (
                where,
                pltpu.make_async_remote_copy(
                    src_ref=source,
                    dst_ref=target,
                    send_sem=halo_send.at[n, slot],
                    recv_sem=halo_recv.at[n, slot],
                    device_id={"frames": col + where[0], "rows": row + where[1]},
                    device_id_type=MESH,
                ),
            )
            for where, source, target, slot in copies
        ]

    def halo_start(n, field):
        edge_s[n, 0] = field[:, 0:128]
        edge_s[n, 1] = field[:, 128:256]
        copies = halo_copies(n)
        start_all(copies[:2])
        wide = [field[g * chunk : (g + 1) * chunk, :] for g in range(GROUPS)]
        packed = dot(jnp.concatenate(wide, axis=1), sel[...]).astype(BF16)
        strip_s[n, 0] = packed[:, 0:128]
        strip_s[n, 1] = packed[:, 128:256]
        start_all(copies[2:])

    def along_columns(n, field):
        if n in CURVATURE:
            cut = rows // 2
            gone, twice = jnp.zeros((cut, 128), BF16), jnp.asarray(2.0, BF16)
            outer = [above[n, 0:cut] * twice, gone], [gone, below[n, cut:rows] * twice]
        else:
            outer = [above[n]], [below[n]]
        stacked = jnp.concatenate(
            [*outer[0], field[:, 0:128], field[:, 128:256], *outer[1]], axis=0
        )
        wide = dot(stacked, band[128:256])
        flat = wide[:, 0:128] + wide[:, 128:256]
        lines = strips[n].reshape(3 * chunk, 256)
        corner = dot(lines, hbh[...]) + dot(lines, hbl[...])

        def part(block, which, h):
            extra = [
                corner[which * chunk : (which + 1) * chunk, g * 256 + h * 128 : g * 256 + h * 128 + 128]
                for g in range(GROUPS)
            ]
            if n in CURVATURE and which != 1:
                gone = jnp.zeros((chunk, 128), F32)
                kept = (0, 1, 2, 3) if which == 0 else (4, 5, 6, 7)
                extra = [2.0 * extra[g] if g in kept else gone for g in range(GROUPS)]
            return flat[block * rows : (block + 1) * rows] + jnp.concatenate(extra, axis=0)

        return [part(0, 0, 1), part(1, 1, 0), part(2, 1, 1), part(3, 2, 0)]

    def smooth(n, field):
        return along_rows(along_columns(n, field))

    def rows_transposed(field):
        result = []
        for q in range(rows // rg):
            tile = field[q * rg : (q + 1) * rg]
            up, same, down = (
                dot(ah[:, d * rg : (d + 1) * rg], tile) + dot(al[:, d * rg : (d + 1) * rg], tile)
                for d in range(3)
            )
            result.append(
                (
                    down[:, 0:128],
                    same[:, 0:128] + down[:, 128:256],
                    up[:, 0:128] + same[:, 128:256],
                    up[:, 128:256],
                )
            )
        return [jnp.concatenate(parts, axis=0) for parts in zip(*result)]

    def smooth_wide(it, buffer):
        blocks = [above_f[it], buffer[:, :, 0], buffer[:, :, 1], below_f[it]]
        blocks = [b.astype(F32).reshape(rows, 128).astype(BF16) for b in blocks]
        step = 8 * per
        gap = jnp.zeros((step, 128), BF16)
        stacked = jnp.concatenate(
            [
                jnp.concatenate(
                    [
                        jnp.concatenate([gap, b[: rows - step]], axis=0),
                        b,
                        jnp.concatenate([b[step:], gap], axis=0),
                    ],
                    axis=1,
                )
                for b in blocks
            ],
            axis=0,
        )
        wide = dot(stacked, band[...])
        flat = wide[:, 0:128] + wide[:, 128:256]
        field = jnp.concatenate(blocks[1:3], axis=1).astype(F32)
        blocks = [flat[b * rows : (b + 1) * rows] for b in range(4)]
        pull_f[it] = REG_WEIGHT * (field - along_rows(blocks))

    def along_rows(blocks):
        pairs = [split(b) for b in blocks]
        result = []
        for q in range(rows // rg):
            cut = slice(q * rg, (q + 1) * rg)

            def tower(which):
                return jnp.concatenate(
                    [
                        jnp.concatenate([pairs[d][which][cut], pairs[d + 1][which][cut]], axis=1)
                        for d in range(3)
                    ],
                    axis=0,
                )

            high = tower(0)
            value = dot(ah[...], high) + dot(al[...], high)
            result.append(value + dot(ah[...], tower(1)))
        return jnp.concatenate(result, axis=0) * scale

    lane = iota((1, 128), 1)

    def sum_start(it, stage, value):
        axis, me, count = (("rows", row, nr), ("frames", col, nf))[stage]
        row_s[it, stage] = value
        row_r[it, stage, pl.ds(me, 1)] = value.reshape(1, 1, 128)

        def send(k, carry):
            pltpu.make_async_remote_copy(
                src_ref=row_s.at[it, stage],
                dst_ref=row_r.at[it, stage, me],
                send_sem=sum_send.at[it, stage],
                recv_sem=sum_recv.at[it, stage],
                device_id={axis: lax.rem(me + k, count)},
                device_id_type=MESH,
            ).start()
            return carry

        lax.fori_loop(1, count, send, 0)

    def sum_end(it, stage):
        count = (nr, nf)[stage]
        wait_bytes(row_r.at[it, stage, pl.ds(0, count - 1)], sum_recv.at[it, stage])
        return jnp.sum(row_r[it, stage], axis=0)

    def total_of(value):
        return jnp.sum(value, keepdims=True)

    recv_all(wide_copies(0, hi_f))
    smooth_wide(0, hi_f)

    def descend(point, pull, back, step):
        return jnp.maximum(point - step * (back + pull) - step * SPARSE_WEIGHT, 0.0)

    def wide_parts(c, h):
        cut = slice(c * 8 * per, (c + 1) * 8 * per)
        return cut, slice(h * 128, (h + 1) * 128)

    def update_first(step):
        wait_bytes(back_f.at[0], a2a_recv.at[3])
        for c in range(nf):
            for h in (0, 1):
                cut, lanes = wide_parts(c, h)
                where = slice(c * 128, (c + 1) * 128)
                point = start_f[:, h, :, where].reshape(8 * per, 128)
                back = back_f[0, c, :, h].astype(F32).reshape(8 * per, 128)
                updated = descend(point, pull_f[0, cut, lanes], back, step).reshape(per, 8, 128)
                first_f[:, h, :, where] = updated
                point_1[c, :, h] = updated.astype(BF16)
        start_all(wide_copies(1, point_1))
        store = pltpu.make_async_copy(first_f, out_first, store_sems.at[0])
        store.start()
        return store

    def slope_last():
        wait_bytes(back_f.at[1], a2a_recv.at[4])
        for c in range(nf):
            for h in (0, 1):
                cut, lanes = wide_parts(c, h)
                back = back_f[1, c, :, h].astype(F32).reshape(8 * per, 128)
                slope = (back + pull_f[1, cut, lanes]).reshape(per, 8, 128)
                slope_f[:, h, :, c * 128 : (c + 1) * 128] = slope
        store = pltpu.make_async_copy(slope_f, out_slope, store_sems.at[1])
        store.start()
        return store

    steps = []
    wait_bytes(hi_c, a2a_recv.at[0])
    point_bf = halves(hi_c).astype(BF16)
    halo_start(0, point_bf)
    to_block(2, lambda c: lo_f.at[c], lo_c)
    for it in range(ITERS):
        now = dot(kw[...], point_bf)
        if it == 0:
            wait_bytes(obs_c, a2a_recv.at[1])
            past = past - halves(obs_c)
        resid_bf = (past + now).astype(BF16)
        back = dot(kwt[...], resid_bf)
        for h in (0, 1):
            part = back[:, h * 128 : (h + 1) * 128].reshape(frames, 8, 128)
            back_c[it, :, h] = part.astype(BF16)
        back = back.astype(BF16).astype(F32)
        if it == 0:
            recv_all(halo_copies(0))
        point_f = point_bf.astype(F32)
        gradient = back + REG_WEIGHT * (point_f - smooth(2 * it, point_bf))
        grad_bf = gradient.astype(BF16)
        halo_start(2 * it + 1, grad_bf)
        back_out(it)
        if it == 0:
            start_all(rest_copies(1))
            halo_start(4, (gradient - grad_bf.astype(F32)).astype(BF16))
        conv = dot(kw[...], grad_bf)
        norm, conv = total_of(gradient * gradient), total_of(conv * conv)
        left = rows_transposed(grad_bf)
        if it == 1:
            store_first = update_first(steps[0])
        recv_all(halo_copies(2 * it + 1))
        right = along_columns(2 * it + 1, grad_bf)
        cross = sum(a * b for a, b in zip(left, right))
        square = grad_bf.astype(F32)
        square = square * square
        curv = total_of(square[:, 0:128] + square[:, 128:256] - scale * cross)
        sum_start(it, 0, jnp.where(lane == 0, norm, jnp.where(lane == 1, conv, curv)))
        if it == 0:
            wait_bytes(lo_c, a2a_recv.at[2])
            low = halves(lo_c)
            halo_start(5, low.astype(BF16))
        else:
            recv_all(wide_copies(1, point_1))
            smooth_wide(1, point_1)
        value = sum_end(it, 0)
        sum_start(it, 1, value)
        if it == 0:
            recv_all(rest_copies(1))
            recv_all(halo_copies(4))
            recv_all(halo_copies(5))
        else:
            store_slope = slope_last()
        value = sum_end(it, 1)
        step = value[:, 0:1] / (value[:, 1:2] + REG_WEIGHT * value[:, 2:3])
        steps.append(step)
        if it == 0:
            point = descend(halves(hi_c) + low, 0.0, gradient, step)
            point_bf = point.astype(BF16)
            for ref in (above, below, strips):
                start, slope = (
                    ref[high].astype(F32) + ref[low_part].astype(F32)
                    for high, low_part in ((0, 5), (1, 4))
                )
                ref[2] = descend(start, 0.0, slope, step).astype(BF16)
    out_step[...] = jnp.broadcast_to(step, out_step.shape)
    store_first.wait()
    store_slope.wait()

    wait_bytes(hi_f.at[pl.ds(0, nf - 1)], a2a_send.at[0])
    wait_bytes(obs_c.at[pl.ds(0, per * (nf - 1))], a2a_send.at[1])
    wait_bytes(lo_f.at[pl.ds(0, nf - 1)], a2a_send.at[2])
    for it in range(ITERS):
        wait_bytes(back_f.at[it, pl.ds(0, nf - 1)], a2a_send.at[3 + it])
        for stage, count in ((0, nr), (1, nf)):
            wait_bytes(row_r.at[it, stage, pl.ds(0, count - 1)], sum_send.at[it, stage])
        send_all(wide_copies(it, hi_f if it == 0 else point_1))
        for n in ((0, 1, 3), (4, 5))[it]:
            send_all(halo_copies(n))
    send_all(rest_copies(1))


def shards(nf, nr, observed, history, spikes_start, kernel, smooth_half):
    per, _, tall, cols = observed.shape
    frames = per * nf
    rows = frames * 8
    hist = history.shape[0]
    assert tall == 16 and history.shape[3] == 128 and cols == 128 * nf
    hist_pad = hist + 1
    rg = min(rows, 256)
    chunk = rows // GROUPS
    most = max(nf, nr)
    block = (per, 2, 8, 128)
    any_spec = pl.BlockSpec(memory_space=pltpu.MemorySpace.HBM)
    vmem = pl.BlockSpec(memory_space=pltpu.VMEM)
    out = jax.ShapeDtypeStruct((per, 2, 8, cols), F32)
    held = functools.partial(pltpu.with_memory_space_constraint, memory_space=pltpu.MemorySpace.HBM)
    first, slope, step = pl.pallas_call(
        functools.partial(body, nf, nr, frames),
        out_shape=(out, out, jax.ShapeDtypeStruct((1, 128), F32)),
        in_specs=[any_spec] * 5,
        out_specs=(any_spec, any_spec, vmem),
        scratch_shapes=[
            pltpu.VMEM((per, 2, 8, cols), F32),
            pltpu.VMEM((nf,) + block, BF16),
            pltpu.VMEM((nf,) + block, BF16),
            pltpu.VMEM((frames, 2, 8, 128), BF16),
            pltpu.VMEM((frames, 2, 8, 128), BF16),
            pltpu.VMEM((frames, 2, 8, 128), BF16),
            pltpu.VMEM((hist_pad, 2, 8, 128), BF16),
            pltpu.VMEM((ITERS, frames, 2, 8, 128), BF16),
            pltpu.VMEM((ITERS, nf) + block, BF16),
            pltpu.VMEM((nf,) + block, BF16),
            pltpu.VMEM((ITERS, nf, per, 8, 128), BF16),
            pltpu.VMEM((ITERS, nf, per, 8, 128), BF16),
            pltpu.VMEM((ITERS, rows, 256), F32),
            pltpu.VMEM((per, 2, 8, cols), F32),
            pltpu.VMEM((per, 2, 8, cols), F32),
            pltpu.SemaphoreType.DMA((2,)),
            pltpu.VMEM((1, kernel.shape[0]), BF16),
            pltpu.SMEM(smooth_half.shape, F32),
            pltpu.VMEM((HALOS, 2, rows, 128), BF16),
            pltpu.VMEM((HALOS, 2, chunk, 128), BF16),
            pltpu.VMEM((HALOS, rows, 128), BF16),
            pltpu.VMEM((HALOS, rows, 128), BF16),
            pltpu.VMEM((HALOS, 3, chunk, 256), BF16),
            pltpu.VMEM((ITERS, 2, 1, 128), F32),
            pltpu.VMEM((ITERS, 2, most, 1, 128), F32),
            pltpu.VMEM((rows, 8 * hist_pad), BF16),
            pltpu.VMEM((rows, rows), BF16),
            pltpu.VMEM((rows, rows), BF16),
            pltpu.VMEM((384, 256), BF16),
            pltpu.VMEM((rg, 3 * rg), BF16),
            pltpu.VMEM((rg, 3 * rg), BF16),
            pltpu.VMEM((GROUPS * 256, 256), BF16),
            pltpu.VMEM((256, GROUPS * 256), BF16),
            pltpu.VMEM((256, GROUPS * 256), BF16),
            pltpu.SemaphoreType.DMA((4,)),
            pltpu.SemaphoreType.DMA((3 + ITERS,)),
            pltpu.SemaphoreType.DMA((3 + ITERS,)),
            pltpu.SemaphoreType.DMA((HALOS, 10)),
            pltpu.SemaphoreType.DMA((HALOS, 10)),
            pltpu.SemaphoreType.DMA((ITERS, 2)),
            pltpu.SemaphoreType.DMA((ITERS, 2)),
            pltpu.SemaphoreType.DMA((ITERS, 2)),
            pltpu.SemaphoreType.DMA((ITERS, 2)),
        ],
        compiler_params=pltpu.CompilerParams(
            collective_id=0, has_side_effects=True, vmem_limit_bytes=44 * 1024 * 1024
        ),
        name="fista",
    )(
        held(observed.reshape(per, 2, 8, cols)),
        held(history.reshape(hist, 2, 8, 128)),
        held(spikes_start.reshape(per, 2, 8, cols)),
        held(kernel.reshape(1, -1)),
        held(smooth_half),
    )
    shape = spikes_start.shape
    step = step[0, 0]
    beta = momentum_terms(ITERS)[-1]
    first, slope = first.reshape(shape), slope.reshape(shape)
    spikes = jnp.maximum(first - step * slope - step * SPARSE_WEIGHT, 0.0)
    return spikes, spikes + beta * (spikes - first)


def solution(mesh):
    in_specs = (
        P("frames", None, "rows", None),
        P(None, None, "rows", "frames"),
        P("frames", None, "rows", None),
        P(),
        P(),
    )
    out_specs = (P("frames", None, "rows", None), P("frames", None, "rows", None))
    step = functools.partial(shards, mesh.shape["frames"], mesh.shape["rows"])
    return jax.shard_map(step, mesh=mesh, in_specs=in_specs, out_specs=out_specs, check_vma=False)
```

```python
import functools
import math

import jax
import jax.numpy as jnp
from jax import lax
from jax.experimental import pallas as pl
from jax.experimental.pallas import tpu as pltpu
from jax.sharding import PartitionSpec as P

ITERS = 2
REG_WEIGHT = 4.0
SPARSE_WEIGHT = 0.1
MESH = pl.DeviceIdType.MESH
F32 = jnp.float32
BF16 = jnp.bfloat16
GROUPS = 8
HALOS = 6
CURVATURE = (1, 3)


def momentum_terms(count):
    current = 1.0
    terms = []
    for iteration in range(count):
        upcoming = (1.0 + math.sqrt(1.0 + 4.0 * current * current)) / 2.0
        terms.append((current - 1.0) / upcoming)
        current = upcoming
    return terms


def iota(shape, dim):
    return lax.broadcasted_iota(jnp.int32, shape, dim)


def dot(a, b):
    return jnp.dot(a, b, preferred_element_type=F32)


def onehot(cond):
    return jnp.where(cond, 1.0, 0.0).astype(BF16)


def split(value):
    high = value.astype(BF16)
    return high, (value - high.astype(F32)).astype(BF16)


def body(
    nf,
    nr,
    frames,
    obs_hbm,
    hist_hbm,
    start_hbm,
    taps_hbm,
    half_hbm,
    out_first,
    out_slope,
    out_step,
    start_f,
    hi_f,
    lo_f,
    hi_c,
    lo_c,
    obs_c,
    hist_v,
    back_c,
    back_f,
    point_1,
    above_f,
    below_f,
    pull_f,
    first_f,
    slope_f,
    store_sems,
    taps_ref,
    half_ref,
    edge_s,
    strip_s,
    above,
    below,
    strips,
    row_s,
    row_r,
    kh,
    kw,
    kwt,
    band,
    ah,
    al,
    sel,
    hbh,
    hbl,
    local_sems,
    a2a_send,
    a2a_recv,
    halo_send,
    halo_recv,
    sum_send,
    sum_recv,
    wide_send,
    wide_recv,
):
    col = lax.axis_index("frames")
    row = lax.axis_index("rows")
    per = frames // nf
    rows = frames * 8
    hist_len = hist_hbm.shape[0]
    tap_count = taps_ref.shape[1]

    load_start = pltpu.make_async_copy(start_hbm, start_f, local_sems.at[0])
    load_start.start()
    load_hist = pltpu.make_async_copy(hist_hbm, hist_v.at[pl.ds(0, hist_len)], local_sems.at[1])
    load_hist.start()
    load_taps = pltpu.make_async_copy(taps_hbm, taps_ref, local_sems.at[2])
    load_taps.start()
    load_half = pltpu.make_async_copy(half_hbm, half_ref, local_sems.at[3])
    load_half.start()

    barrier = pltpu.get_barrier_semaphore()

    def signal_frames(k, carry):
        pl.semaphore_signal(
            barrier, inc=1, device_id={"frames": lax.rem(col + k, nf)}, device_id_type=MESH
        )
        return carry

    def signal_rows(k, carry):
        pl.semaphore_signal(
            barrier, inc=1, device_id={"rows": lax.rem(row + k, nr)}, device_id_type=MESH
        )
        return carry

    lax.fori_loop(1, nf, signal_frames, 0)
    lax.fori_loop(1, nr, signal_rows, 0)
    exists = {}
    for dc in (-1, 0, 1):
        for dr in (-1, 0, 1):
            conds = []
            if dc == -1:
                conds.append(col > 0)
            if dc == 1:
                conds.append(col < nf - 1)
            if dr == -1:
                conds.append(row > 0)
            if dr == 1:
                conds.append(row < nr - 1)
            if conds:
                exists[dc, dr] = functools.reduce(jnp.logical_and, conds)
    for dc in (-1, 1):
        for dr in (-1, 1):

            @pl.when(exists[dc, dr])
            def _():
                pl.semaphore_signal(
                    barrier,
                    inc=1,
                    device_id={"frames": col + dc, "rows": row + dr},
                    device_id_type=MESH,
                )

    load_start.wait()
    for c in range(nf):
        high, low = split(start_f[:, :, :, c * 128 : (c + 1) * 128])
        hi_f[c] = high
        lo_f[c] = low

    sides = (col > 0).astype(jnp.int32) + (col < nf - 1).astype(jnp.int32)
    ends = (row > 0).astype(jnp.int32) + (row < nr - 1).astype(jnp.int32)
    pl.semaphore_wait(barrier, (nf - 1) + (nr - 1) + sides * ends)

    def order(k):
        return nf // 2 + ((k + 1) // 2) * (1 - 2 * lax.rem(k, 2))

    def exchange(index, source, target, own_source, own_target):
        own = pltpu.make_async_copy(own_source, own_target, a2a_recv.at[index])
        own.start()

        def send(k, carry):
            peer = lax.rem(col + order(k), nf)
            pltpu.make_async_remote_copy(
                src_ref=source(peer),
                dst_ref=target,
                send_sem=a2a_send.at[index],
                recv_sem=a2a_recv.at[index],
                device_id={"frames": peer},
                device_id_type=MESH,
            ).start()
            return carry

        lax.fori_loop(0, nf - 1, send, 0)

    def wait_bytes(view, sem):
        pltpu.make_async_copy(view, view, sem).wait()

    def to_block(index, source, buffer):
        target = buffer.at[pl.ds(col * per, per)]
        exchange(index, source, target, source(col), target)

    to_block(0, lambda c: hi_f.at[c], hi_c)
    to_block(1, lambda c: obs_hbm.at[:, :, :, pl.ds(pl.multiple_of(c * 128, 128), 128)], obs_c)

    def back_out(it):
        target = back_f.at[it, col]
        exchange(
            3 + it,
            lambda f: back_c.at[it, pl.ds(f * per, per)],
            target,
            back_c.at[it, pl.ds(col * per, per)],
            target,
        )

    def wide_copies(it, buffer):
        copies = [((0, -1), 0, below_f), ((0, 1), 1, above_f)]
        return [
            (
                where,
                pltpu.make_async_remote_copy(
                    src_ref=buffer.at[:, :, h],
                    dst_ref=target.at[it],
                    send_sem=wide_send.at[it, h],
                    recv_sem=wide_recv.at[it, h],
                    device_id={"rows": row + where[1]},
                    device_id_type=MESH,
                ),
            )
            for where, h, target in copies
        ]

    def start_all(copies):
        for where, copy in copies:

            @pl.when(exists[where])
            def _():
                copy.start()

    def recv_all(copies):
        for where, copy in copies:

            @pl.when(exists[-where[0], -where[1]])
            def _():
                copy.wait_recv()

    def send_all(copies):
        for where, copy in copies:

            @pl.when(exists[where])
            def _():
                copy.wait_send()

    start_all(wide_copies(0, hi_f))

    def clear(ref):
        ref[...] = jnp.zeros(ref.shape, BF16)

    @pl.when(row == 0)
    def _():
        clear(above)
        clear(above_f)
        clear(strips.at[:, 0])

    @pl.when(row == nr - 1)
    def _():
        clear(below)
        clear(below_f)
        clear(strips.at[:, 2])

    @pl.when(col == 0)
    def _():
        clear(strips.at[:, :, :, pl.ds(0, 128)])

    @pl.when(col == nf - 1)
    def _():
        clear(strips.at[:, :, :, pl.ds(128, 128)])

    hist_v[hist_len:] = jnp.zeros((hist_v.shape[0] - hist_len,) + hist_v.shape[1:], BF16)

    size = 256
    load_taps.wait()
    load_half.wait()
    spread = jnp.concatenate(
        [taps_ref[...].astype(F32), jnp.zeros((1, size - tap_count), F32)], axis=1
    )
    spread = jnp.broadcast_to(spread, (size, size))
    shifted = pltpu.roll(spread, size - (tap_count - 1), 1, stride=1, stride_axis=0).astype(BF16)
    at_t = onehot(iota((rows, size), 0) // 8 == iota((rows, size), 1))
    by_s = lax.dot_general(
        at_t, shifted, (((1,), (1,)), ((), ())), preferred_element_type=F32
    ).astype(BF16)

    def same_row(shape):
        return lax.rem(iota(shape, 0), 8) == lax.rem(iota(shape, 1), 8)

    hist_cols = kh.shape[1]
    s_of = iota((size, hist_cols), 0)
    pick = onehot((s_of == iota((size, hist_cols), 1) // 8) & (s_of < hist_len))
    kh[...] = jnp.where(same_row((rows, hist_cols)), dot(by_s, pick), 0.0).astype(BF16)
    pick = onehot(iota((size, rows), 0) == iota((size, rows), 1) // 8 + hist_len)
    kw[...] = jnp.where(same_row((rows, rows)), dot(by_s, pick), 0.0).astype(BF16)
    at_s = onehot(iota((rows, size), 0) // 8 + hist_len == iota((rows, size), 1))
    by_t = dot(at_s, shifted).astype(BF16)
    pick = onehot(iota((size, rows), 0) == iota((size, rows), 1) // 8)
    kwt[...] = jnp.where(same_row((rows, rows)), dot(by_t, pick), 0.0).astype(BF16)

    half = [half_ref[k] for k in range(half_ref.shape[0])]
    reach = half_ref.shape[0] - 1
    total = half[0]
    for k in range(1, reach + 1):
        total = total + 2.0 * half[k]
    total = jnp.full((1, 1), total, F32)
    scale = 1.0 / (total * total)

    def taps_at(distance):
        value = jnp.zeros(distance.shape, F32)
        for k in range(reach + 1):
            value = jnp.where(distance == k, half[k], value)
        return value

    high, low = split(taps_at(jnp.abs(iota((384, 128), 0) - 128 - iota((384, 128), 1))))
    band[:, 0:128] = high
    band[:, 128:256] = low

    rg = ah.shape[0]
    i0, i1 = iota((rg, rg), 0), iota((rg, rg), 1)
    for d in (-1, 0, 1):
        near = taps_at(jnp.abs(8 * d + lax.rem(i1, 8) - lax.rem(i0, 8)))
        high, low = split(jnp.where(i0 // 8 == i1 // 8, near, 0.0))
        ah[:, (d + 1) * rg : (d + 2) * rg] = high
        al[:, (d + 1) * rg : (d + 2) * rg] = low

    k0, k1 = iota((256, 256), 0), iota((256, 256), 1)
    place = lax.rem(k0, 128)
    inner, line = lax.rem(place, 8), lax.rem(k1, 128)
    near = taps_at(jnp.where(k0 < 128, line + 8 - inner, 128 + inner - line))
    near = jnp.where(lax.rem(place // 8, 2) == k1 // 128, near, 0.0)
    for g in range(GROUPS):
        high, low = split(jnp.where(place // 16 == g, near, 0.0))
        hbh[:, g * 256 : (g + 1) * 256] = high
        hbl[:, g * 256 : (g + 1) * 256] = low
    place = lax.rem(k1, 128)
    inner, line = lax.rem(place, 8), lax.rem(k0, 128)
    chosen = (lax.rem(place // 8, 2) == k0 // 128) & (line == jnp.where(k1 < 128, 120 + inner, inner))
    for g in range(GROUPS):
        sel[g * 256 : (g + 1) * 256, :] = onehot(chosen & (place // 16 == g))

    def halves(ref):
        parts = [ref[:, h].astype(F32).reshape(rows, 128) for h in (0, 1)]
        return jnp.concatenate(parts, axis=1)

    load_hist.wait()
    past = [hist_v[:, h].astype(F32).reshape(hist_cols, 128) for h in (0, 1)]
    past = dot(kh[...], jnp.concatenate(past, axis=1).astype(BF16))

    chunk = rows // GROUPS

    def edge_rows(n):
        cut = rows // 2 if n in CURVATURE else rows
        return pl.ds(0, cut), pl.ds(rows - cut, cut)

    def edge_copy(n, dr, part, slot):
        source, target = (edge_s.at[n, 0], below) if dr == -1 else (edge_s.at[n, 1], above)
        return (
            (0, dr),
            pltpu.make_async_remote_copy(
                src_ref=source.at[part],
                dst_ref=target.at[n, part],
                send_sem=halo_send.at[n, slot],
                recv_sem=halo_recv.at[n, slot],
                device_id={"rows": row + dr},
                device_id_type=MESH,
            ),
        )

    def rest_copies(n):
        half_rows = rows // 2
        return [
            edge_copy(n, -1, pl.ds(0, half_rows), 8),
            edge_copy(n, 1, pl.ds(half_rows, half_rows), 9),
        ]

    def halo_copies(n):
        upper, lower = edge_rows(n)
        result = [edge_copy(n, -1, lower, 1), edge_copy(n, 1, upper, 0)]
        copies = []
        for dc in (-1, 1):
            side = 0 if dc == 1 else 1
            for dr in (-1, 0, 1):
                copies.append(
                    (
                        (dc, dr),
                        strip_s.at[n, side],
                        strips.at[n, 1 - dr, :, pl.ds(side * 128, 128)],
                        2 + side * 3 + 1 - dr,
                    )
                )
        return result + [
            (
                where,
                pltpu.make_async_remote_copy(
                    src_ref=source,
                    dst_ref=target,
                    send_sem=halo_send.at[n, slot],
                    recv_sem=halo_recv.at[n, slot],
                    device_id={"frames": col + where[0], "rows": row + where[1]},
                    device_id_type=MESH,
                ),
            )
            for where, source, target, slot in copies
        ]

    def halo_start(n, field):
        edge_s[n, 0] = field[:, 0:128]
        edge_s[n, 1] = field[:, 128:256]
        copies = halo_copies(n)
        start_all(copies[:2])
        wide = [field[g * chunk : (g + 1) * chunk, :] for g in range(GROUPS)]
        packed = dot(jnp.concatenate(wide, axis=1), sel[...]).astype(BF16)
        strip_s[n, 0] = packed[:, 0:128]
        strip_s[n, 1] = packed[:, 128:256]
        start_all(copies[2:])

    def columns_inside(stacked):
        wide = dot(stacked, band[128:256])
        return wide[:, 0:128] + wide[:, 128:256]

    def own_columns(field):
        return columns_inside(jnp.concatenate([field[:, 0:128], field[:, 128:256]], axis=0))

    def along_columns(n, own):
        if n in CURVATURE:
            cut = rows // 2
            gone, twice = jnp.zeros((cut, 128), BF16), jnp.asarray(2.0, BF16)
            outer = [above[n, 0:cut] * twice, gone], [gone, below[n, cut:rows] * twice]
        else:
            outer = [above[n]], [below[n]]
        outside = columns_inside(jnp.concatenate([*outer[0], *outer[1]], axis=0))
        flat = jnp.concatenate([outside[:rows], own, outside[rows:]], axis=0)
        lines = strips[n].reshape(3 * chunk, 256)
        corner = dot(lines, hbh[...]) + dot(lines, hbl[...])

        def part(block, which, h):
            extra = [
                corner[which * chunk : (which + 1) * chunk, g * 256 + h * 128 : g * 256 + h * 128 + 128]
                for g in range(GROUPS)
            ]
            if n in CURVATURE and which != 1:
                gone = jnp.zeros((chunk, 128), F32)
                kept = (0, 1, 2, 3) if which == 0 else (4, 5, 6, 7)
                extra = [2.0 * extra[g] if g in kept else gone for g in range(GROUPS)]
            return flat[block * rows : (block + 1) * rows] + jnp.concatenate(extra, axis=0)

        return [part(0, 0, 1), part(1, 1, 0), part(2, 1, 1), part(3, 2, 0)]

    def smooth(n, field):
        return along_rows(along_columns(n, own_columns(field)))

    def rows_transposed(field):
        result = []
        for q in range(rows // rg):
            tile = field[q * rg : (q + 1) * rg]
            up, same, down = (
                dot(ah[:, d * rg : (d + 1) * rg], tile) + dot(al[:, d * rg : (d + 1) * rg], tile)
                for d in range(3)
            )
            result.append(
                (
                    down[:, 0:128],
                    same[:, 0:128] + down[:, 128:256],
                    up[:, 0:128] + same[:, 128:256],
                    up[:, 128:256],
                )
            )
        return [jnp.concatenate(parts, axis=0) for parts in zip(*result)]

    def smooth_wide(it, buffer):
        blocks = [above_f[it], buffer[:, :, 0], buffer[:, :, 1], below_f[it]]
        blocks = [b.astype(F32).reshape(rows, 128).astype(BF16) for b in blocks]
        step = 8 * per
        gap = jnp.zeros((step, 128), BF16)
        stacked = jnp.concatenate(
            [
                jnp.concatenate(
                    [
                        jnp.concatenate([gap, b[: rows - step]], axis=0),
                        b,
                        jnp.concatenate([b[step:], gap], axis=0),
                    ],
                    axis=1,
                )
                for b in blocks
            ],
            axis=0,
        )
        wide = dot(stacked, band[...])
        flat = wide[:, 0:128] + wide[:, 128:256]
        field = jnp.concatenate(blocks[1:3], axis=1).astype(F32)
        blocks = [flat[b * rows : (b + 1) * rows] for b in range(4)]
        pull_f[it] = REG_WEIGHT * (field - along_rows(blocks))

    def along_rows(blocks):
        pairs = [split(b) for b in blocks]
        result = []
        for q in range(rows // rg):
            cut = slice(q * rg, (q + 1) * rg)

            def tower(which):
                return jnp.concatenate(
                    [
                        jnp.concatenate([pairs[d][which][cut], pairs[d + 1][which][cut]], axis=1)
                        for d in range(3)
                    ],
                    axis=0,
                )

            high = tower(0)
            value = dot(ah[...], high) + dot(al[...], high)
            result.append(value + dot(ah[...], tower(1)))
        return jnp.concatenate(result, axis=0) * scale

    lane = iota((1, 128), 1)

    def sum_start(it, stage, value):
        axis, me, count = (("rows", row, nr), ("frames", col, nf))[stage]
        row_s[it, stage] = value
        row_r[it, stage, pl.ds(me, 1)] = value.reshape(1, 1, 128)

        def send(k, carry):
            pltpu.make_async_remote_copy(
                src_ref=row_s.at[it, stage],
                dst_ref=row_r.at[it, stage, me],
                send_sem=sum_send.at[it, stage],
                recv_sem=sum_recv.at[it, stage],
                device_id={axis: lax.rem(me + k, count)},
                device_id_type=MESH,
            ).start()
            return carry

        lax.fori_loop(1, count, send, 0)

    def sum_end(it, stage):
        count = (nr, nf)[stage]
        wait_bytes(row_r.at[it, stage, pl.ds(0, count - 1)], sum_recv.at[it, stage])
        return jnp.sum(row_r[it, stage], axis=0)

    def total_of(value):
        return jnp.sum(value, keepdims=True)

    recv_all(wide_copies(0, hi_f))
    smooth_wide(0, hi_f)

    def descend(point, pull, back, step):
        return jnp.maximum(point - step * (back + pull) - step * SPARSE_WEIGHT, 0.0)

    def wide_parts(c, h):
        cut = slice(c * 8 * per, (c + 1) * 8 * per)
        return cut, slice(h * 128, (h + 1) * 128)

    def update_first(step):
        wait_bytes(back_f.at[0], a2a_recv.at[3])
        for c in range(nf):
            for h in (0, 1):
                cut, lanes = wide_parts(c, h)
                where = slice(c * 128, (c + 1) * 128)
                point = start_f[:, h, :, where].reshape(8 * per, 128)
                back = back_f[0, c, :, h].astype(F32).reshape(8 * per, 128)
                updated = descend(point, pull_f[0, cut, lanes], back, step).reshape(per, 8, 128)
                first_f[:, h, :, where] = updated
                point_1[c, :, h] = updated.astype(BF16)
        start_all(wide_copies(1, point_1))
        store = pltpu.make_async_copy(first_f, out_first, store_sems.at[0])
        store.start()
        return store

    def slope_last():
        wait_bytes(back_f.at[1], a2a_recv.at[4])
        for c in range(nf):
            for h in (0, 1):
                cut, lanes = wide_parts(c, h)
                back = back_f[1, c, :, h].astype(F32).reshape(8 * per, 128)
                slope = (back + pull_f[1, cut, lanes]).reshape(per, 8, 128)
                slope_f[:, h, :, c * 128 : (c + 1) * 128] = slope
        store = pltpu.make_async_copy(slope_f, out_slope, store_sems.at[1])
        store.start()
        return store

    steps = []
    wait_bytes(hi_c, a2a_recv.at[0])
    point_bf = halves(hi_c).astype(BF16)
    halo_start(0, point_bf)
    to_block(2, lambda c: lo_f.at[c], lo_c)
    for it in range(ITERS):
        now = dot(kw[...], point_bf)
        if it == 0:
            wait_bytes(obs_c, a2a_recv.at[1])
            past = past - halves(obs_c)
        resid_bf = (past + now).astype(BF16)
        back = dot(kwt[...], resid_bf)
        for h in (0, 1):
            part = back[:, h * 128 : (h + 1) * 128].reshape(frames, 8, 128)
            back_c[it, :, h] = part.astype(BF16)
        back = back.astype(BF16).astype(F32)
        if it == 0:
            recv_all(halo_copies(0))
        point_f = point_bf.astype(F32)
        gradient = back + REG_WEIGHT * (point_f - smooth(2 * it, point_bf))
        grad_bf = gradient.astype(BF16)
        halo_start(2 * it + 1, grad_bf)
        back_out(it)
        if it == 0:
            start_all(rest_copies(1))
            halo_start(4, (gradient - grad_bf.astype(F32)).astype(BF16))
        conv = dot(kw[...], grad_bf)
        norm, conv = total_of(gradient * gradient), total_of(conv * conv)
        left = rows_transposed(grad_bf)
        own = own_columns(grad_bf)
        if it == 1:
            store_first = update_first(steps[0])
        recv_all(halo_copies(2 * it + 1))
        right = along_columns(2 * it + 1, own)
        cross = sum(a * b for a, b in zip(left, right))
        square = grad_bf.astype(F32)
        square = square * square
        curv = total_of(square[:, 0:128] + square[:, 128:256] - scale * cross)
        sum_start(it, 0, jnp.where(lane == 0, norm, jnp.where(lane == 1, conv, curv)))
        if it == 0:
            wait_bytes(lo_c, a2a_recv.at[2])
            low = halves(lo_c)
            halo_start(5, low.astype(BF16))
        else:
            recv_all(wide_copies(1, point_1))
            smooth_wide(1, point_1)
        value = sum_end(it, 0)
        sum_start(it, 1, value)
        if it == 0:
            recv_all(rest_copies(1))
            recv_all(halo_copies(4))
            recv_all(halo_copies(5))
        else:
            store_slope = slope_last()
        value = sum_end(it, 1)
        step = value[:, 0:1] / (value[:, 1:2] + REG_WEIGHT * value[:, 2:3])
        steps.append(step)
        if it == 0:
            point = descend(halves(hi_c) + low, 0.0, gradient, step)
            point_bf = point.astype(BF16)
            for ref in (above, below, strips):
                start, slope = (
                    ref[high].astype(F32) + ref[low_part].astype(F32)
                    for high, low_part in ((0, 5), (1, 4))
                )
                ref[2] = descend(start, 0.0, slope, step).astype(BF16)
    out_step[...] = jnp.broadcast_to(step, out_step.shape)
    store_first.wait()
    store_slope.wait()

    wait_bytes(hi_f.at[pl.ds(0, nf - 1)], a2a_send.at[0])
    wait_bytes(obs_c.at[pl.ds(0, per * (nf - 1))], a2a_send.at[1])
    wait_bytes(lo_f.at[pl.ds(0, nf - 1)], a2a_send.at[2])
    for it in range(ITERS):
        wait_bytes(back_f.at[it, pl.ds(0, nf - 1)], a2a_send.at[3 + it])
        for stage, count in ((0, nr), (1, nf)):
            wait_bytes(row_r.at[it, stage, pl.ds(0, count - 1)], sum_send.at[it, stage])
        send_all(wide_copies(it, hi_f if it == 0 else point_1))
        for n in ((0, 1, 3), (4, 5))[it]:
            send_all(halo_copies(n))
    send_all(rest_copies(1))


def shards(nf, nr, observed, history, spikes_start, kernel, smooth_half):
    per, _, tall, cols = observed.shape
    frames = per * nf
    rows = frames * 8
    hist = history.shape[0]
    assert tall == 16 and history.shape[3] == 128 and cols == 128 * nf
    hist_pad = hist + 1
    rg = min(rows, 256)
    chunk = rows // GROUPS
    most = max(nf, nr)
    block = (per, 2, 8, 128)
    any_spec = pl.BlockSpec(memory_space=pltpu.MemorySpace.HBM)
    vmem = pl.BlockSpec(memory_space=pltpu.VMEM)
    out = jax.ShapeDtypeStruct((per, 2, 8, cols), F32)
    held = functools.partial(pltpu.with_memory_space_constraint, memory_space=pltpu.MemorySpace.HBM)
    first, slope, step = pl.pallas_call(
        functools.partial(body, nf, nr, frames),
        out_shape=(out, out, jax.ShapeDtypeStruct((1, 128), F32)),
        in_specs=[any_spec] * 5,
        out_specs=(any_spec, any_spec, vmem),
        scratch_shapes=[
            pltpu.VMEM((per, 2, 8, cols), F32),
            pltpu.VMEM((nf,) + block, BF16),
            pltpu.VMEM((nf,) + block, BF16),
            pltpu.VMEM((frames, 2, 8, 128), BF16),
            pltpu.VMEM((frames, 2, 8, 128), BF16),
            pltpu.VMEM((frames, 2, 8, 128), BF16),
            pltpu.VMEM((hist_pad, 2, 8, 128), BF16),
            pltpu.VMEM((ITERS, frames, 2, 8, 128), BF16),
            pltpu.VMEM((ITERS, nf) + block, BF16),
            pltpu.VMEM((nf,) + block, BF16),
            pltpu.VMEM((ITERS, nf, per, 8, 128), BF16),
            pltpu.VMEM((ITERS, nf, per, 8, 128), BF16),
            pltpu.VMEM((ITERS, rows, 256), F32),
            pltpu.VMEM((per, 2, 8, cols), F32),
            pltpu.VMEM((per, 2, 8, cols), F32),
            pltpu.SemaphoreType.DMA((2,)),
            pltpu.VMEM((1, kernel.shape[0]), BF16),
            pltpu.SMEM(smooth_half.shape, F32),
            pltpu.VMEM((HALOS, 2, rows, 128), BF16),
            pltpu.VMEM((HALOS, 2, chunk, 128), BF16),
            pltpu.VMEM((HALOS, rows, 128), BF16),
            pltpu.VMEM((HALOS, rows, 128), BF16),
            pltpu.VMEM((HALOS, 3, chunk, 256), BF16),
            pltpu.VMEM((ITERS, 2, 1, 128), F32),
            pltpu.VMEM((ITERS, 2, most, 1, 128), F32),
            pltpu.VMEM((rows, 8 * hist_pad), BF16),
            pltpu.VMEM((rows, rows), BF16),
            pltpu.VMEM((rows, rows), BF16),
            pltpu.VMEM((384, 256), BF16),
            pltpu.VMEM((rg, 3 * rg), BF16),
            pltpu.VMEM((rg, 3 * rg), BF16),
            pltpu.VMEM((GROUPS * 256, 256), BF16),
            pltpu.VMEM((256, GROUPS * 256), BF16),
            pltpu.VMEM((256, GROUPS * 256), BF16),
            pltpu.SemaphoreType.DMA((4,)),
            pltpu.SemaphoreType.DMA((3 + ITERS,)),
            pltpu.SemaphoreType.DMA((3 + ITERS,)),
            pltpu.SemaphoreType.DMA((HALOS, 10)),
            pltpu.SemaphoreType.DMA((HALOS, 10)),
            pltpu.SemaphoreType.DMA((ITERS, 2)),
            pltpu.SemaphoreType.DMA((ITERS, 2)),
            pltpu.SemaphoreType.DMA((ITERS, 2)),
            pltpu.SemaphoreType.DMA((ITERS, 2)),
        ],
        compiler_params=pltpu.CompilerParams(
            collective_id=0, has_side_effects=True, vmem_limit_bytes=44 * 1024 * 1024
        ),
        name="fista",
    )(
        held(observed.reshape(per, 2, 8, cols)),
        held(history.reshape(hist, 2, 8, 128)),
        held(spikes_start.reshape(per, 2, 8, cols)),
        held(kernel.reshape(1, -1)),
        held(smooth_half),
    )
    shape = spikes_start.shape
    step = step[0, 0]
    beta = momentum_terms(ITERS)[-1]
    first, slope = first.reshape(shape), slope.reshape(shape)
    spikes = jnp.maximum(first - step * slope - step * SPARSE_WEIGHT, 0.0)
    return spikes, spikes + beta * (spikes - first)


def solution(mesh):
    in_specs = (
        P("frames", None, "rows", None),
        P(None, None, "rows", "frames"),
        P("frames", None, "rows", None),
        P(),
        P(),
    )
    out_specs = (P("frames", None, "rows", None), P("frames", None, "rows", None))
    step = functools.partial(shards, mesh.shape["frames"], mesh.shape["rows"])
    return jax.shard_map(step, mesh=mesh, in_specs=in_specs, out_specs=out_specs, check_vma=False)
```
